32 devices in a mesh: fourier: 8 (over y, x, core), mer: 4 (over z).
Axes of the slice: x: 2, y: 2, z: 4, core: 2. Of those that a mesh axis runs over, the one named last changes fastest.
Arguments:
- velocity: float32 [3, 256, 64, 1024], P(None, 'fourier', None, 'mer')
- metrics: float32 [4, 64, 1024], P(None, None, 'mer'), may hold values from -0.3 to 0.3
- lumped_mass: float32 [64, 1024], P(None, 'mer'), may hold values from 0.5 to 2
- element_ops: float32 [64, 64, 1024], P(None, None, 'mer'), may hold values from -0.75 to 0.75
- boundary_map: int32 [1024, 28], P('mer'), may hold values from 0 to 13311, as said below
- block_cols: int32 [104, 4], P('mer'), may hold values from 0 to 103, as said below
- schur_blocks: float32 [104, 4, 128, 128], P('mer'), may hold values from -0.25 to 0.25
Outputs:
- element_out: float32 [3, 256, 64, 1024], P(None, 'fourier', None, 'mer')
- boundary_out: float32 [3, 256, 13312], P(None, 'fourier', 'mer')
The draws below stay inside these ranges and needn't reach their ends.
Inputs may be any that keep to these rules, and one draw needn't show every extreme that they name: `boundary_map`: every entry of an element of slab s (elements s * 256 to (s + 1) * 256 - 1) lies from s * 3328 to (s + 1) * 3328 + 127, and for the last slab below (s + 1) * 3328; both ends are taken in every slab. `block_cols`: entry s of row r differs from r by at most 2; entry 0 is r itself.
All inputs are finite; a program needn't handle non-finite values.
Results may differ from the reference program's by a relative error of at most 0.00014.
Values sent between devices are 32-bit elements; how exact they have to be, the bound alone decides.
No kernel may reach another device: no remote copies, remote signals or barrier semaphores. Data moves between devices by JAX's collectives and lax.ppermute only.
A program may use at most 192 MiB of HBM per device.

```python
import math
import jax
import jax.numpy as jnp
import numpy as np
from jax import lax

NP = 64
PERIM = 28
K = 256
E_DEV = 256
BS = 128
HB = 2
NNZ = 4
ELEMS = 1024
BOUND_DEV = 3328
RIM = 128
BOUND = 13312
BLOCKS = 104


def draw_velocity(key, part):
    index = jnp.arange(K)
    wave = jnp.where(index == K - 1, K // 2, (index + 1) // 2).astype(jnp.float32)
    amplitude = 1.0 / (1.0 + wave / 16.0)
    base = jax.random.normal(key, (3, K, NP, ELEMS), jnp.float32)
    return base * amplitude[None, :, None, None]


def draw_boundary_map(key, part):
    element = jnp.arange(ELEMS)[:, None]
    point = jnp.arange(PERIM)[None, :]
    slab = element // E_DEV
    local = element % E_DEV
    last_slab = ELEMS // E_DEV - 1
    lower = slab * BOUND_DEV
    upper = jnp.where(slab == last_slab, lower + BOUND_DEV, lower + BOUND_DEV + RIM)
    span = upper - lower
    raw = jax.random.randint(key, (ELEMS, PERIM), 0, 1 << 30)
    values = lower + raw % span
    values = jnp.where((local == E_DEV - 1) & (point == PERIM - 1), upper - 1, values)
    values = jnp.where((local == 0) & (point == 0), lower, values)
    return values.astype(jnp.int32)


def draw_block_cols(key, part):
    row = jnp.arange(BLOCKS)[:, None]
    slot = jnp.arange(NNZ)[None, :]
    offset = jax.random.randint(key, (BLOCKS, NNZ), -HB, HB + 1)
    offset = jnp.where(slot == 0, 0, jnp.where(slot == 1, -HB, jnp.where(slot == 2, HB, offset)))
    return jnp.clip(row + offset, 0, BLOCKS - 1).astype(jnp.int32)


def shard_levels(stream_key, dims, shards, low, high):
    def one(dim, shards_of):
        steps = jax.random.uniform(jax.random.fold_in(jax.random.fold_in(stream_key, 6), dim), (shards_of,), jnp.float32, low / len(shards), high / len(shards))
        return jnp.repeat(jnp.exp(steps), dims[dim] // shards_of).reshape((-1,) + (1,) * (len(dims) - dim - 1))

    level = one(*shards[0])
    for cut in shards[1:]:
        level = level * one(*cut)
    return level


def centred(rng, shape, width, reach, cuts=(), held_as=jnp.bfloat16):
    level = shard_levels(rng, shape, cuts, -0.22, 0.18) if cuts else 1.0
    values = jax.random.normal(rng, shape, jnp.float32) * width * level
    return jnp.minimum(jnp.maximum(values, -reach), reach).astype(held_as)


def setup_inputs(seed: int = 0) -> dict:
    key_list = jax.random.split(jax.random.key(seed), 8)
    velocity = draw_velocity(jax.random.fold_in(key_list[7], 71), 0)
    metrics = jnp.clip(jax.random.uniform(key_list[1], (4, NP, ELEMS), jnp.float32, -0.3, 0.3) * shard_levels(key_list[1], (4, NP, ELEMS), ((2, 4),), -0.4, 0.0), -0.3, 0.3)
    lumped_mass = jnp.clip(jnp.exp(math.log(2.0) - 1.3862944 * jax.random.uniform(key_list[2], (NP, ELEMS), jnp.float32) ** shard_levels(key_list[2], (NP, ELEMS), ((1, 4),), -0.2, 0.2)), 0.5, 2.0)
    element_ops = centred(key_list[3], (NP, NP, ELEMS), NP ** -0.5, 0.75, ((2, 4),), jnp.float32)
    boundary_map = draw_boundary_map(jax.random.fold_in(key_list[7], 71), 0)
    block_cols = draw_block_cols(jax.random.fold_in(key_list[7], 71), 0)
    schur_blocks = centred(key_list[6], (BLOCKS, NNZ, BS, BS), (NNZ * BS) ** -0.5, 0.25, ((0, 4),), jnp.float32)
    return {"velocity": velocity, "metrics": metrics, "lumped_mass": lumped_mass, "element_ops": element_ops, "boundary_map": boundary_map, "block_cols": block_cols, "schur_blocks": schur_blocks}


gauss_nodes = [-1.0, -0.8717401485096066, -0.5917001814331423, -0.2092992179024789, 0.2092992179024789, 0.5917001814331423, 0.8717401485096066, 1.0]
wave_scale = 1.0 / 32.0


def node_tables():
    nodes = np.array(gauss_nodes)
    count = nodes.shape[0]
    barycentric = np.array([1.0 / np.prod([nodes[i] - nodes[k] for k in range(count) if k != i]) for i in range(count)])
    matrix = np.zeros((count, count))
    for i in range(count):
        for j in range(count):
            if i != j:
                matrix[i, j] = barycentric[j] / barycentric[i] / (nodes[i] - nodes[j])
        matrix[i, i] = -np.sum(matrix[i])
    return np.kron(matrix, np.eye(count)), np.kron(np.eye(count), matrix)


def perimeter_points():
    points = [8 * a + b for a in range(8) for b in range(8) if a in (0, 7) or b in (0, 7)]
    return np.array(points, dtype=np.int32)


def spectral_tables(modes):
    planes = 3 * modes // 2
    index = np.arange(modes)
    wave = np.where(index == modes - 1, modes // 2, (index + 1) // 2)
    is_sine = (index % 2 == 0) & (index > 0) & (index < modes - 1)
    theta = 2.0 * np.pi * np.arange(planes) / planes
    angle = theta[:, None] * wave[None, :]
    basis = np.where(is_sine[None, :], np.sin(angle), np.cos(angle))
    deriv = wave_scale * wave[None, :] * np.where(is_sine[None, :], np.cos(angle), -np.sin(angle))
    weight = np.where(index == 0, 1.0, 2.0) / planes
    back = (basis * weight[None, :]).T
    return basis, deriv, back, wave


def reference(velocity, metrics, lumped_mass, element_ops, boundary_map, block_cols, schur_blocks):
    high = lax.Precision.HIGHEST
    basis, deriv, back, wave = spectral_tables(K)
    forward_table = jnp.asarray(basis, jnp.float32)
    deriv_table = jnp.asarray(deriv, jnp.float32)
    back_table = jnp.asarray(back, jnp.float32)
    deriv_r_np, deriv_s_np = node_tables()
    deriv_r = jnp.asarray(deriv_r_np, jnp.float32)
    deriv_s = jnp.asarray(deriv_s_np, jnp.float32)
    nblocks = ELEMS // E_DEV

    def split(array):
        shaped = array.reshape(array.shape[:-1] + (nblocks, E_DEV))
        return jnp.moveaxis(shaped, -2, 0)

    def one_block(items):
        block_vel, block_met = items
        planes = jnp.einsum('jk,fkpe->fjpe', forward_table, block_vel, precision=high)
        grad_z = jnp.einsum('jk,fkpe->fjpe', deriv_table, block_vel, precision=high)
        along_r = jnp.einsum('qp,fjpe->fjqe', deriv_r, planes, precision=high)
        along_s = jnp.einsum('qp,fjpe->fjqe', deriv_s, planes, precision=high)
        grad_x = block_met[0] * along_r + block_met[2] * along_s
        grad_y = block_met[1] * along_r + block_met[3] * along_s
        advection = -(planes[0:1] * grad_x + planes[1:2] * grad_y + planes[2:3] * grad_z)
        return jnp.einsum('kj,fjpe->fkpe', back_table, advection, precision=high)

    projected = lax.map(one_block, (split(velocity), split(metrics)))
    projected = jnp.moveaxis(projected, 0, -2).reshape(velocity.shape)
    forcing = velocity + projected
    helm = 1.0 + 4.0 * (jnp.asarray(wave, jnp.float32) / (K / 2)) ** 2
    element_out = jnp.einsum('ije,fkje->fkie', element_ops, forcing, precision=high)
    element_out = element_out + helm[None, :, None, None] * lumped_mass[None, None] * forcing
    perim = perimeter_points()
    values = element_out[:, :, perim, :]
    values = jnp.transpose(values, (3, 2, 0, 1)).reshape(ELEMS * PERIM, 3 * K)
    ids = boundary_map.reshape(-1).astype(jnp.int32)
    assembled = jax.ops.segment_sum(values, ids, num_segments=BOUND)
    blocked = assembled.T.reshape(3 * K, BLOCKS, BS)
    picked = blocked[:, block_cols, :]
    result = jnp.einsum('rsab,frsb->fra', schur_blocks, picked, precision=high)
    boundary_out = result.reshape(3, K, BOUND)
    return element_out, boundary_out
```

```python
import functools

import jax
import jax.numpy as jnp
import numpy as np
from jax import lax
from jax.experimental import pallas as pl
from jax.experimental.pallas import tpu as pltpu
from jax.sharding import PartitionSpec as P

K = 256
HB = 2
NP = 64
ORDER = 8
LANES = 128
SUB = LANES // ORDER
WIDE = 256
COLS = NP * SUB


gauss_nodes = [
    -1.0,
    -0.8717401485096066,
    -0.5917001814331423,
    -0.2092992179024789,
    0.2092992179024789,
    0.5917001814331423,
    0.8717401485096066,
    1.0,
]
wave_scale = 1.0 / 32.0


def node_matrix():
    nodes = np.array(gauss_nodes)
    count = nodes.shape[0]
    barycentric = np.array(
        [1.0 / np.prod([nodes[i] - nodes[k] for k in range(count) if k != i]) for i in range(count)]
    )
    matrix = np.zeros((count, count))
    for i in range(count):
        for j in range(count):
            if i != j:
                matrix[i, j] = barycentric[j] / barycentric[i] / (nodes[i] - nodes[j])
        matrix[i, i] = -np.sum(matrix[i])
    return matrix


perimeter = [8 * a + b for a in range(8) for b in range(8) if a in (0, 7) or b in (0, 7)]
PERIM = len(perimeter)


def spectral_tables(modes):
    planes = 3 * modes // 2
    index = np.arange(modes)
    wave = np.where(index == modes - 1, modes // 2, (index + 1) // 2)
    is_sine = (index % 2 == 0) & (index > 0) & (index < modes - 1)
    theta = 2.0 * np.pi * np.arange(planes) / planes
    angle = theta[:, None] * wave[None, :]
    basis = np.where(is_sine[None, :], np.sin(angle), np.cos(angle))
    deriv = wave_scale * wave[None, :] * np.where(is_sine[None, :], np.cos(angle), -np.sin(angle))
    weight = np.where(index == 0, 1.0, 2.0) / planes
    back = (basis * weight[None, :]).T
    return (basis, deriv, back, wave)


def halves(table):
    table = np.asarray(table, np.float32)
    high = table.astype(jnp.bfloat16)
    low = (table - high.astype(np.float32)).astype(jnp.bfloat16)
    return jnp.asarray(high), jnp.asarray(low)


def split(value):
    high = value.astype(jnp.bfloat16)
    low = (value - high.astype(jnp.float32)).astype(jnp.bfloat16)
    return high, low


def dot(left, right):
    return jnp.dot(left, right, preferred_element_type=jnp.float32)


def dot_nt(left, right):
    return lax.dot_general(left, right, (((1,), (1,)), ((), ())), preferred_element_type=jnp.float32)


def lane_groups_swapped(rows):
    rows = list(rows)
    lane = lax.broadcasted_iota(jnp.int32, rows[0].shape, 1)
    for step in (4, 2, 1):
        lower = (lane & (step * SUB)) == 0
        for i in range(ORDER):
            if i & step:
                continue
            top, bottom = rows[i], rows[i + step]
            rows[i] = jnp.where(lower, top, pltpu.roll(bottom, step * SUB, 1))
            rows[i + step] = jnp.where(lower, pltpu.roll(top, LANES - step * SUB, 1), bottom)
    return rows


def pack_kernel(modes, v_ref, o_ref):
    for a in range(ORDER):
        rows = [v_ref[pl.ds(ORDER * a + b, modes, stride=NP), :] for b in range(ORDER)]
        for g, row in enumerate(lane_groups_swapped(rows)):
            o_ref[g, :, a * LANES : (a + 1) * LANES] = row


def pack(v2, chunk, tiles, modes, groups):
    return pl.pallas_call(
        functools.partial(pack_kernel, modes),
        out_shape=jax.ShapeDtypeStruct((groups, modes, 3 * COLS), jnp.float32),
        grid=(3, tiles),
        in_specs=[pl.BlockSpec((modes * NP, LANES), lambda f, t: (f, chunk * tiles + t))],
        out_specs=pl.BlockSpec((ORDER, modes, COLS), lambda f, t: (t, 0, f)),
        compiler_params=pltpu.CompilerParams(vmem_limit_bytes=24 << 20),
        cost_estimate=pl.CostEstimate(flops=0, transcendentals=0, bytes_accessed=8 * 3 * tiles * modes * NP * LANES),
        name="pack",
    )(v2)


def physics_kernel(planes, even, odd, x_ref, fh_ref, fl_ref, wh_ref, wl_ref, bh_ref, bl_ref, m_ref, y_ref,
                   p_ref, z_ref, s_ref, ah_ref, al_ref):
    width = 3 * COLS

    def forward(tile, carry):
        cols = pl.ds(pl.multiple_of(tile * WIDE, WIDE), WIDE)
        xh, xl = split(x_ref[:, cols])
        fh = fh_ref[...]
        both = dot(fh, xh) + dot(fl_ref[...], xh) + dot(fh, xl)
        values = both[:planes]
        p_ref[:, cols] = values
        z_ref[:, cols] = both[planes:]
        ph, plo = split(values)
        wh = wh_ref[...]
        s_ref[:, cols] = dot(ph, wh) + dot(plo, wh) + dot(ph, wl_ref[...])
        return carry

    lax.fori_loop(0, width // WIDE, forward, 0)

    step = 16

    def products(tile, carry):
        rows = pl.ds(pl.multiple_of(tile * step, step), step)

        def piece(ref, f, a):
            start = f * COLS + a * LANES
            return ref[rows, start : start + LANES]

        speed_r, speed_s, speed_z = [], [], []
        for a in range(ORDER):
            p0, p1, p2 = (piece(p_ref, f, a) for f in range(3))
            m0, m1, m2, m3 = (m_ref[ORDER * q + a : ORDER * q + a + 1, :] for q in range(4))
            speed_r.append(p0 * m0 + p1 * m1)
            speed_s.append(p0 * m2 + p1 * m3)
            speed_z.append(p2)
        for f in range(3):
            values = [piece(p_ref, f, a) for a in range(ORDER)]
            total = [values[j] + values[7 - j] for j in range(4)]
            diff = [values[j] - values[7 - j] for j in range(4)]
            for i in range(4):
                e = even[i][0] * total[0]
                o = odd[i][0] * diff[0]
                for j in range(1, 4):
                    e = e + even[i][j] * total[j]
                    o = o + odd[i][j] * diff[j]
                for a, along in ((i, o + e), (7 - i, o - e)):
                    out = speed_r[a] * along + speed_s[a] * piece(s_ref, f, a) + speed_z[a] * piece(z_ref, f, a)
                    high, low = split(out)
                    start = f * COLS + a * LANES
                    ah_ref[rows, start : start + LANES] = high
                    al_ref[rows, start : start + LANES] = low
        return carry

    lax.fori_loop(0, planes // step, products, 0)

    def backward(tile, carry):
        cols = pl.ds(pl.multiple_of(tile * WIDE, WIDE), WIDE)
        ah = ah_ref[:, cols]
        bh = bh_ref[...]
        y_ref[:, cols] = dot(bh, ah) + dot(bl_ref[...], ah) + dot(bh, al_ref[:, cols])
        return carry

    lax.fori_loop(0, width // WIDE, backward, 0)


def physics(received, metrics):
    basis, deriv, back, _ = spectral_tables(K)
    planes = basis.shape[0]
    width = 3 * COLS
    fh, fl = halves(np.concatenate([basis, deriv], axis=0))
    bh, bl = halves(-back)
    matrix = node_matrix()
    wh, wl = halves(np.kron(np.eye(WIDE // LANES), np.kron(matrix.T, np.eye(SUB))))
    flipped = matrix[:, ::-1]
    even = ((matrix + flipped) / 2)[:4, :4].astype(np.float32).tolist()
    odd = ((matrix - flipped) / 2)[:4, :4].astype(np.float32).tolist()
    return pl.pallas_call(
        functools.partial(physics_kernel, planes, even, odd),
        out_shape=jax.ShapeDtypeStruct((K, width), jnp.float32),
        in_specs=[pl.BlockSpec(memory_space=pltpu.VMEM)] * 8,
        out_specs=pl.BlockSpec(memory_space=pltpu.VMEM),
        scratch_shapes=[pltpu.VMEM((planes, width), jnp.float32)] * 3
        + [pltpu.VMEM((planes, width), jnp.bfloat16)] * 2,
        compiler_params=pltpu.CompilerParams(vmem_limit_bytes=48 << 20),
        cost_estimate=pl.CostEstimate(
            flops=6 * planes * width * (3 * K + WIDE), transcendentals=0, bytes_accessed=8 * K * width
        ),
        name="physics",
    )(received, fh, fl, wh, wl, bh, bl, metrics)


def element_kernel(modes, aliased, v_ref, r_ref, a_ref, mass_ref, helm_ref, *refs):
    o_ref, pv_ref, f_ref = refs[1:] if aliased else refs
    for a in range(ORDER):
        rows = [r_ref[g, :, a * LANES : (a + 1) * LANES] for g in range(ORDER)]
        for b, row in enumerate(lane_groups_swapped(rows)):
            p = ORDER * a + b
            f_ref[p] = v_ref[pl.ds(p, modes, stride=NP), :] + row

    block = 4

    def op_rows(tile, carry):
        first = tile * block
        sums = []
        for q in range(block):
            i = first + q
            sums.append(helm_ref[...] * mass_ref[pl.ds(i, 1), :] * f_ref[i])
        for j in range(NP):
            value = f_ref[j]
            for q in range(block):
                sums[q] = sums[q] + a_ref[pl.ds((first + q) * NP + j, 1), :] * value
        for q in range(block):
            o_ref[pl.ds(first + q, modes, stride=NP), :] = sums[q]
        return carry

    lax.fori_loop(0, NP // block, op_rows, 0)
    for t, p in enumerate(perimeter):
        pv_ref[:, t * LANES : (t + 1) * LANES] = o_ref[pl.ds(p, modes, stride=NP), :]


def element_stage(v2, received, ops2, mass, helm, previous, chunk, tiles, modes):
    aliased = previous is not None
    in_specs = [
        pl.BlockSpec((modes * NP, LANES), lambda t, f: (f, chunk * tiles + t)),
        pl.BlockSpec((ORDER, modes, COLS), lambda t, f: (t, 0, f)),
        pl.BlockSpec((NP * NP, LANES), lambda t, f: (0, chunk * tiles + t)),
        pl.BlockSpec((NP, LANES), lambda t, f: (0, chunk * tiles + t)),
        pl.BlockSpec((modes, LANES), lambda t, f: (0, 0)),
    ]
    args = [v2, received, ops2, mass, helm]
    if aliased:
        in_specs.append(pl.BlockSpec(memory_space=pl.ANY))
        args.append(previous)
    return pl.pallas_call(
        functools.partial(element_kernel, modes, aliased),
        out_shape=(
            jax.ShapeDtypeStruct(v2.shape, jnp.float32),
            jax.ShapeDtypeStruct((3 * modes, tiles * PERIM * LANES), jnp.float32),
        ),
        grid=(tiles, 3),
        in_specs=in_specs,
        out_specs=(
            pl.BlockSpec((modes * NP, LANES), lambda t, f: (f, chunk * tiles + t)),
            pl.BlockSpec((modes, PERIM * LANES), lambda t, f: (f, t)),
        ),
        scratch_shapes=[pltpu.VMEM((NP, modes, LANES), jnp.float32)],
        input_output_aliases={5: 0} if aliased else {},
        compiler_params=pltpu.CompilerParams(vmem_limit_bytes=32 << 20),
        cost_estimate=pl.CostEstimate(
            flops=2 * 3 * tiles * modes * NP * NP * LANES, transcendentals=0,
            bytes_accessed=4 * 4 * 3 * tiles * modes * NP * LANES,
        ),
        name="element",
    )(*args)


def assemble_kernel(rows, first, *refs):
    if first:
        pv_ref, ids_ref, o_ref, lhs_ref = refs
    else:
        pv_ref, ids_ref, before_ref, o_ref, lhs_ref = refs

    @pl.when(pl.program_id(0) == 0)
    def _():
        high, low = split(pv_ref[...])
        lhs_ref[:rows] = high
        lhs_ref[rows:] = low

    depth = pv_ref.shape[1]
    wanted = lax.broadcasted_iota(jnp.int32, (WIDE, LANES), 1) + pl.program_id(0) * WIDE
    total = jnp.zeros((2 * rows, WIDE), jnp.float32)
    for start in range(0, depth, WIDE):
        ids = ids_ref[start : start + WIDE, :]
        hot = [
            jnp.where(ids == wanted + LANES * h, 1.0, 0.0).astype(jnp.bfloat16)
            for h in range(WIDE // LANES)
        ]
        total = total + dot(lhs_ref[:, start : start + WIDE], jnp.concatenate(hot, axis=1))
    total = total[:rows] + total[rows:]
    o_ref[...] = total if first else before_ref[...] + total


def assemble(values, ids, before, width):
    rows, depth = values.shape
    first = before is None
    in_specs = [pl.BlockSpec(memory_space=pltpu.VMEM)] * 2
    args = [values, ids]
    if not first:
        in_specs.append(pl.BlockSpec((rows, WIDE), lambda n: (0, n)))
        args.append(before)
    return pl.pallas_call(
        functools.partial(assemble_kernel, rows, first),
        out_shape=jax.ShapeDtypeStruct((rows, width), jnp.float32),
        grid=(width // WIDE,),
        in_specs=in_specs,
        out_specs=pl.BlockSpec((rows, WIDE), lambda n: (0, n)),
        scratch_shapes=[pltpu.VMEM((2 * rows, depth), jnp.bfloat16)],
        compiler_params=pltpu.CompilerParams(vmem_limit_bytes=32 << 20),
        cost_estimate=pl.CostEstimate(
            flops=4 * rows * depth * width, transcendentals=0, bytes_accessed=4 * (2 * rows + LANES) * depth
        ),
        name="assemble",
    )(*args)


def coupling_kernel(cols_ref, x_ref, b_ref, o_ref, xh_ref, xl_ref):
    r = pl.program_id(0)

    @pl.when(r == 0)
    def _():
        high, low = split(x_ref[...])
        xh_ref[...] = high
        xl_ref[...] = low

    total = jnp.zeros(o_ref.shape, jnp.float32)
    for s in range(b_ref.shape[1]):
        at = pl.ds(pl.multiple_of(cols_ref[r, s] * LANES, LANES), LANES)
        bh, bl = split(b_ref[0, s])
        xh = xh_ref[:, at]
        total = total + dot_nt(xh, bh) + dot_nt(xl_ref[:, at], bh) + dot_nt(xh, bl)
    o_ref[...] = total


def coupling(extended, local_cols, blocks):
    rows = extended.shape[0]
    count, slots, size, _ = blocks.shape
    return pl.pallas_call(
        coupling_kernel,
        out_shape=jax.ShapeDtypeStruct((rows, count * size), jnp.float32),
        grid_spec=pltpu.PrefetchScalarGridSpec(
            num_scalar_prefetch=1,
            grid=(count,),
            in_specs=[
                pl.BlockSpec(extended.shape, lambda r, c: (0, 0)),
                pl.BlockSpec((1, slots, size, size), lambda r, c: (r, 0, 0, 0)),
            ],
            out_specs=pl.BlockSpec((rows, size), lambda r, c: (0, r)),
            scratch_shapes=[pltpu.VMEM(extended.shape, jnp.bfloat16)] * 2,
        ),
        compiler_params=pltpu.CompilerParams(vmem_limit_bytes=32 << 20),
        cost_estimate=pl.CostEstimate(
            flops=6 * rows * slots * size * size * count, transcendentals=0,
            bytes_accessed=4 * slots * size * size * count,
        ),
        name="coupling",
    )(local_cols, extended, blocks)


def per_device(velocity, metrics, lumped_mass, element_ops, boundary_map, block_cols, schur_blocks):
    modes, elems = velocity.shape[1], velocity.shape[3]
    groups = lax.axis_size("fourier")
    part = lax.axis_index("fourier")
    slab = lax.axis_index("mer")
    slabs = lax.axis_size("mer")
    block_rows, block_size = schur_blocks.shape[0], schur_blocks.shape[2]
    owned_count = block_rows * block_size
    tiles = groups // ORDER
    chunks = elems // (tiles * LANES)

    v2 = velocity.reshape(3 * modes * NP, elems)
    ops2 = element_ops.reshape(NP * NP, elems)
    wave = jnp.asarray(spectral_tables(K)[3], jnp.float32)
    local_wave = lax.dynamic_slice_in_dim(wave, part * modes, modes)
    helm = 1.0 + 4.0 * (local_wave / (K / 2)) ** 2
    helm = jnp.broadcast_to(helm[:, None], (modes, LANES))
    ids = boundary_map - slab * owned_count
    ids = ids.reshape(chunks, tiles, LANES, PERIM).transpose(0, 1, 3, 2).reshape(chunks, -1)
    ids = jnp.broadcast_to(ids[:, :, None], ids.shape + (LANES,))
    width = -(-(owned_count + block_size) // WIDE) * WIDE

    returned = []
    for chunk in range(chunks):
        sent = pack(v2, chunk, tiles, modes, groups)
        got = lax.all_to_all(sent, "fourier", split_axis=0, concat_axis=0, tiled=True)
        first = (chunk * tiles + part // ORDER) * LANES + (part % ORDER) * SUB
        local_metrics = lax.dynamic_slice_in_dim(metrics, first, SUB, 2).reshape(4 * ORDER, LANES)
        projected = physics(got.reshape(K, 3 * COLS), local_metrics)
        back = lax.all_to_all(
            projected.reshape(groups, modes, 3 * COLS), "fourier", split_axis=0, concat_axis=0, tiled=True
        )
        returned.append(back)

    out, sums = None, None
    for chunk in range(chunks):
        out, values = element_stage(v2, returned[chunk], ops2, lumped_mass, helm, out, chunk, tiles, modes)
        sums = assemble(values, ids[chunk], sums, width)

    reach = HB * block_size
    up = [(i, i + 1) for i in range(slabs - 1)]
    down = [(i + 1, i) for i in range(slabs - 1)]
    from_below = lax.ppermute(sums[:, owned_count - reach : owned_count + block_size], "mer", up)
    from_above = lax.ppermute(sums[:, :reach], "mer", down)
    start = sums[:, :block_size] + from_below[:, reach:]
    after = from_above[:, :block_size] + sums[:, owned_count : owned_count + block_size]
    extended = jnp.concatenate(
        [from_below[:, :reach], start, sums[:, block_size:owned_count], after, from_above[:, block_size:]], axis=1
    )
    local_cols = block_cols - slab * block_rows + HB
    boundary_out = coupling(extended, local_cols, schur_blocks)
    return (out.reshape(velocity.shape), boundary_out.reshape(3, modes, owned_count))


def solution(mesh):
    in_specs = (
        P(None, "fourier", None, "mer"),
        P(None, None, "mer"),
        P(None, "mer"),
        P(None, None, "mer"),
        P("mer", None),
        P("mer", None),
        P("mer", None, None, None),
    )
    out_specs = (P(None, "fourier", None, "mer"), P(None, "fourier", "mer"))
    return jax.shard_map(
        per_device, mesh=mesh, in_specs=in_specs, out_specs=out_specs, check_vma=False
    )
```

```python
import functools

import jax
import jax.numpy as jnp
import numpy as np
from jax import lax
from jax.experimental import pallas as pl
from jax.experimental.pallas import tpu as pltpu
from jax.sharding import PartitionSpec as P

K = 256
HB = 2
NP = 64
ORDER = 8
LANES = 128
SUB = LANES // ORDER
WIDE = 256
COLS = NP * SUB
PERIM = 28
VMEM_LIMIT = 61 << 20
ASSEMBLED = 512


gauss_nodes = [
    -1.0,
    -0.8717401485096066,
    -0.5917001814331423,
    -0.2092992179024789,
    0.2092992179024789,
    0.5917001814331423,
    0.8717401485096066,
    1.0,
]
wave_scale = 1.0 / 32.0


def node_matrix():
    nodes = np.array(gauss_nodes)
    count = nodes.shape[0]
    barycentric = np.array(
        [1.0 / np.prod([nodes[i] - nodes[k] for k in range(count) if k != i]) for i in range(count)]
    )
    matrix = np.zeros((count, count))
    for i in range(count):
        for j in range(count):
            if i != j:
                matrix[i, j] = barycentric[j] / barycentric[i] / (nodes[i] - nodes[j])
        matrix[i, i] = -np.sum(matrix[i])
    return matrix


def spectral_tables(modes):
    planes = 3 * modes // 2
    index = np.arange(modes)
    wave = np.where(index == modes - 1, modes // 2, (index + 1) // 2)
    is_sine = (index % 2 == 0) & (index > 0) & (index < modes - 1)
    theta = 2.0 * np.pi * np.arange(planes) / planes
    angle = theta[:, None] * wave[None, :]
    basis = np.where(is_sine[None, :], np.sin(angle), np.cos(angle))
    deriv = wave_scale * wave[None, :] * np.where(is_sine[None, :], np.cos(angle), -np.sin(angle))
    weight = np.where(index == 0, 1.0, 2.0) / planes
    back = (basis * weight[None, :]).T
    return (basis, deriv, back, wave)


def halves(table):
    table = np.asarray(table, np.float32)
    high = table.astype(jnp.bfloat16)
    low = (table - high.astype(np.float32)).astype(jnp.bfloat16)
    return jnp.asarray(high), jnp.asarray(low)


def split(value):
    high = value.astype(jnp.bfloat16)
    low = (value - high.astype(jnp.float32)).astype(jnp.bfloat16)
    return high, low


def dot(left, right):
    return jnp.dot(left, right, preferred_element_type=jnp.float32)


def dot_nt(left, right):
    return lax.dot_general(left, right, (((1,), (1,)), ((), ())), preferred_element_type=jnp.float32)


def groups_picked(rows):
    lane = lax.broadcasted_iota(jnp.int32, rows[0].shape, 1)
    for step in (4, 2, 1):
        upper = (lane & (step * SUB)) != 0
        rows = [jnp.where(upper, rows[(i + step) % ORDER], rows[i]) for i in range(ORDER)]
    return [rows[-g % ORDER] for g in range(ORDER)]


def rolled(row, groups):
    shift = groups % ORDER * SUB
    return pltpu.roll(row, shift, 1) if shift else row


def pack_kernel(modes, v_ref, o_ref):
    for a in range(ORDER):
        rows = [v_ref[pl.ds(ORDER * a + b, modes, stride=NP), :] for b in range(ORDER)]
        rows = groups_picked([rolled(row, b) for b, row in enumerate(rows)])
        for g, row in enumerate(rows):
            o_ref[g, :, a * LANES : (a + 1) * LANES] = row


def pack(v2, chunk, tiles, modes, groups):
    return pl.pallas_call(
        functools.partial(pack_kernel, modes),
        out_shape=jax.ShapeDtypeStruct((groups, modes, 3 * COLS), jnp.float32),
        grid=(3, tiles),
        in_specs=[pl.BlockSpec((modes * NP, LANES), lambda f, t: (f, chunk * tiles + t))],
        out_specs=pl.BlockSpec((ORDER, modes, COLS), lambda f, t: (t, 0, f)),
        compiler_params=pltpu.CompilerParams(vmem_limit_bytes=VMEM_LIMIT),
        cost_estimate=pl.CostEstimate(flops=0, transcendentals=0, bytes_accessed=8 * 3 * tiles * modes * NP * LANES),
        name="pack",
    )(v2)


def physics_kernel(planes, even, odd, counts, fh_ref, fl_ref, wh_ref, wl_ref, bh_ref, bl_ref, m_ref, x_hbm, *refs):
    outs = refs[: len(counts)]
    x_ref, y_ref, p_ref, z_ref, s_ref, ah_ref, al_ref, in_sem, out_sem = refs[len(counts) :]
    width = 3 * COLS

    def arriving(tile):
        cols = pl.ds(pl.multiple_of(tile * WIDE, WIDE), WIDE)
        return pltpu.make_async_copy(x_hbm.at[:, cols], x_ref.at[:, cols], in_sem.at[tile])

    for tile in range(width // WIDE):
        arriving(tile).start()

    def forward(tile, carry):
        cols = pl.ds(pl.multiple_of(tile * WIDE, WIDE), WIDE)
        arriving(tile).wait()
        xh, xl = split(x_ref[:, cols])
        fh = fh_ref[...]
        both = dot(fh, xh) + dot(fl_ref[...], xh) + dot(fh, xl)
        values = both[:planes]
        p_ref[:, cols] = values
        z_ref[:, cols] = both[planes:]
        ph, plo = split(values)
        wh = wh_ref[...]
        s_ref[:, cols] = dot(ph, wh) + dot(plo, wh) + dot(ph, wl_ref[...])
        return carry

    lax.fori_loop(0, width // WIDE, forward, 0)

    step = 16

    def products(tile, carry):
        rows = pl.ds(pl.multiple_of(tile * step, step), step)

        def piece(ref, f, a):
            start = f * COLS + a * LANES
            return ref[rows, start : start + LANES]

        speed_r, speed_s, speed_z = [], [], []
        for a in range(ORDER):
            p0, p1, p2 = (piece(p_ref, f, a) for f in range(3))
            m0, m1, m2, m3 = (m_ref[ORDER * q + a : ORDER * q + a + 1, :] for q in range(4))
            speed_r.append(p0 * m0 + p1 * m1)
            speed_s.append(p0 * m2 + p1 * m3)
            speed_z.append(p2)
        for f in range(3):
            values = [piece(p_ref, f, a) for a in range(ORDER)]
            total = [values[j] + values[7 - j] for j in range(4)]
            diff = [values[j] - values[7 - j] for j in range(4)]
            for i in range(4):
                e = even[i][0] * total[0]
                o = odd[i][0] * diff[0]
                for j in range(1, 4):
                    e = e + even[i][j] * total[j]
                    o = o + odd[i][j] * diff[j]
                for a, along in ((i, o + e), (7 - i, o - e)):
                    out = speed_r[a] * along + speed_s[a] * piece(s_ref, f, a) + speed_z[a] * piece(z_ref, f, a)
                    high, low = split(out)
                    start = f * COLS + a * LANES
                    ah_ref[rows, start : start + LANES] = high
                    al_ref[rows, start : start + LANES] = low
        return carry

    lax.fori_loop(0, planes // step, products, 0)

    def backward(tile, carry):
        cols = pl.ds(pl.multiple_of(tile * WIDE, WIDE), WIDE)
        ah = ah_ref[:, cols]
        bh = bh_ref[...]
        y_ref[:, cols] = dot(bh, ah) + dot(bl_ref[...], ah) + dot(bh, al_ref[:, cols])
        return carry

    start, leaving = 0, []
    for n, count in enumerate(counts):
        stop = start + count * COLS
        lax.fori_loop(start // WIDE, stop // WIDE, backward, 0)
        leaving.append(pltpu.make_async_copy(y_ref.at[:, start:stop], outs[n], out_sem.at[n]))
        leaving[-1].start()
        start = stop
    for copy in leaving:
        copy.wait()


def physics(received, turn, metrics, counts):
    basis, deriv, back, _ = spectral_tables(K)
    planes = basis.shape[0]
    width = 3 * COLS
    fh, fl = halves(np.concatenate([basis, deriv], axis=0))
    bh, bl = halves(-back)
    matrix = node_matrix()
    metrics = jnp.roll(metrics, turn * SUB, 1)
    wh, wl = (jnp.roll(table, (turn, turn), (0, 1)) for table in halves(matrix.T))
    spread = [jnp.eye(n, dtype=jnp.bfloat16) for n in (WIDE // LANES, SUB)]
    wh, wl = (
        jnp.einsum("xy,bc,ef->xbeycf", spread[0], table, spread[1]).reshape(WIDE, WIDE) for table in (wh, wl)
    )
    flipped = matrix[:, ::-1]
    even = ((matrix + flipped) / 2)[:4, :4].astype(np.float32).tolist()
    odd = ((matrix - flipped) / 2)[:4, :4].astype(np.float32).tolist()
    return pl.pallas_call(
        functools.partial(physics_kernel, planes, even, odd, counts),
        out_shape=[jax.ShapeDtypeStruct((K, count * COLS), jnp.float32) for count in counts],
        in_specs=[pl.BlockSpec(memory_space=pltpu.VMEM)] * 7 + [pl.BlockSpec(memory_space=pl.ANY)],
        out_specs=[pl.BlockSpec(memory_space=pl.ANY)] * len(counts),
        scratch_shapes=[pltpu.VMEM((K, width), jnp.float32)] * 2
        + [pltpu.VMEM((planes, width), jnp.float32)] * 3
        + [pltpu.VMEM((planes, width), jnp.bfloat16)] * 2
        + [pltpu.SemaphoreType.DMA((width // WIDE,)), pltpu.SemaphoreType.DMA((len(counts),))],
        compiler_params=pltpu.CompilerParams(vmem_limit_bytes=VMEM_LIMIT),
        cost_estimate=pl.CostEstimate(
            flops=6 * planes * width * (3 * K + WIDE), transcendentals=0, bytes_accessed=8 * K * width
        ),
        name="physics",
    )(fh, fl, wh, wl, bh, bl, metrics, received)


def sublane_groups_swapped(rows):
    rows = list(rows)
    line = lax.broadcasted_iota(jnp.int32, (ORDER, LANES), 0)
    for step in (4, 2, 1):
        lower = (line & step) == 0
        for i in range(ORDER):
            if i & step:
                continue
            top, bottom = rows[i], rows[i + step]
            rows[i] = jnp.where(lower, top, pltpu.roll(bottom, step, 0))
            rows[i + step] = jnp.where(lower, pltpu.roll(top, ORDER - step, 0), bottom)
    return rows


def element_kernel(modes, aliased, v_ref, r_ref, a_ref, mass_ref, helm_ref, *refs):
    o_ref, high_ref, low_ref, f_ref = refs[1:] if aliased else refs
    bands = modes // ORDER
    for a in range(ORDER):
        rows = groups_picked([r_ref[g, :, a * LANES : (a + 1) * LANES] for g in range(ORDER)])
        rows = [rolled(row, -b) for b, row in enumerate(rows)]
        for u in range(bands):
            own = sublane_groups_swapped([v_ref[ORDER * u + k, a * ORDER : (a + 1) * ORDER, :] for k in range(ORDER)])
            for b in range(ORDER):
                f_ref[ORDER * a + b, ORDER * u : ORDER * (u + 1), :] = own[b] + rows[b][ORDER * u : ORDER * (u + 1), :]

    def op_rows(a, carry):
        first = pl.multiple_of(a * ORDER, ORDER)
        sums = []
        for b in range(ORDER):
            weight = helm_ref[...] * mass_ref[a, b : b + 1, :]
            own = f_ref[first + b]
            sums.append([(weight * own)[ORDER * u : ORDER * (u + 1), :] for u in range(bands)])
        for j in range(NP):
            value = f_ref[j]
            for b in range(ORDER):
                weight = a_ref[first + b, j : j + 1, :]
                for u in range(bands):
                    sums[b][u] = sums[b][u] + weight * value[ORDER * u : ORDER * (u + 1), :]

        def keep(b, slot):
            at = pl.ds(pl.multiple_of(slot * LANES, LANES), LANES)
            high, low = split(jnp.concatenate(sums[b], axis=0))
            high_ref[:, at] = high
            low_ref[:, at] = low

        keep(0, 2 * a)
        keep(ORDER - 1, 2 * a + 1)

        @pl.when((a == 0) | (a == ORDER - 1))
        def _():
            for b in range(1, ORDER - 1):
                keep(b, 2 * ORDER + jnp.where(a == 0, 0, ORDER - 2) + b - 1)

        for u in range(bands):
            rows = sublane_groups_swapped([sums[b][u] for b in range(ORDER)])
            for k in range(ORDER):
                o_ref[ORDER * u + k, pl.ds(first, ORDER), :] = rows[k]
        return carry

    lax.fori_loop(0, ORDER, op_rows, 0)


kept = [8 * a + b for a in range(8) for b in (0, 7)] + [8 * a + b for a in (0, 7) for b in range(1, 7)]


def element_stage(v3, received, ops, mass, helm, previous, chunk, tiles, modes, first):
    count = received.shape[2] // COLS
    aliased = previous is not None
    in_specs = [
        pl.BlockSpec((modes, NP, LANES), lambda t, f: (first + f, 0, chunk * tiles + t)),
        pl.BlockSpec((ORDER, modes, COLS), lambda t, f: (t, 0, f)),
        pl.BlockSpec((NP, NP, LANES), lambda t, f: (0, 0, chunk * tiles + t)),
        pl.BlockSpec((ORDER, ORDER, LANES), lambda t, f: (0, 0, chunk * tiles + t)),
        pl.BlockSpec((modes, LANES), lambda t, f: (0, 0)),
    ]
    args = [v3, received, ops, mass, helm]
    if aliased:
        in_specs.append(pl.BlockSpec(memory_space=pl.ANY))
        args.append(previous)
    values = jax.ShapeDtypeStruct((count * modes, tiles * PERIM * LANES), jnp.bfloat16)
    values_spec = pl.BlockSpec((modes, PERIM * LANES), lambda t, f: (f, t))
    return pl.pallas_call(
        functools.partial(element_kernel, modes, aliased),
        out_shape=(jax.ShapeDtypeStruct(v3.shape, jnp.float32), values, values),
        grid=(tiles, count),
        in_specs=in_specs,
        out_specs=(
            pl.BlockSpec((modes, NP, LANES), lambda t, f: (first + f, 0, chunk * tiles + t)),
            values_spec,
            values_spec,
        ),
        scratch_shapes=[pltpu.VMEM((NP, modes, LANES), jnp.float32)],
        input_output_aliases={5: 0} if aliased else {},
        compiler_params=pltpu.CompilerParams(vmem_limit_bytes=VMEM_LIMIT),
        cost_estimate=pl.CostEstimate(
            flops=2 * count * tiles * modes * NP * NP * LANES, transcendentals=0,
            bytes_accessed=4 * 4 * count * tiles * modes * NP * LANES,
        ),
        name="element",
    )(*args)


def assemble_kernel(parts, block, *refs):
    ids_ref, o_ref = refs[2 * parts], refs[-1]
    rows, depth = o_ref.shape[0], refs[0].shape[1]
    wanted = lax.broadcasted_iota(jnp.int32, (WIDE, LANES), 1) + pl.program_id(0) * block
    total = jnp.zeros((2 * rows, block), jnp.float32)
    for start in range(0, depth, WIDE):
        ids = ids_ref[start : start + WIDE, :] - wanted
        hot = [jnp.where(ids == LANES * h, 1.0, 0.0).astype(jnp.bfloat16) for h in range(block // LANES)]
        values = jnp.concatenate([ref[:, start : start + WIDE] for ref in refs[: 2 * parts]], axis=0)
        total = total + dot(values, jnp.concatenate(hot, axis=1))
    total = total[:rows] + total[rows:]
    o_ref[...] = total if len(refs) == 2 * parts + 2 else refs[-2][...] + total


def assemble(values, ids, before, width, block=ASSEMBLED):
    highs, lows = zip(*values)
    rows, depth = sum(high.shape[0] for high in highs), highs[0].shape[1]
    in_specs = [pl.BlockSpec(memory_space=pltpu.VMEM)] * (2 * len(values) + 1)
    args = [*highs, *lows, ids]
    if before is not None:
        in_specs.append(pl.BlockSpec((rows, block), lambda n: (0, n)))
        args.append(before)
    return pl.pallas_call(
        functools.partial(assemble_kernel, len(values), block),
        out_shape=jax.ShapeDtypeStruct((rows, width), jnp.float32),
        grid=(width // block,),
        in_specs=in_specs,
        out_specs=pl.BlockSpec((rows, block), lambda n: (0, n)),
        compiler_params=pltpu.CompilerParams(vmem_limit_bytes=32 << 20),
        cost_estimate=pl.CostEstimate(
            flops=4 * rows * depth * width, transcendentals=0, bytes_accessed=4 * (2 * rows + LANES) * depth
        ),
        name="assemble",
    )(*args)


def coupling_kernel(pair, cols_ref, at_ref, x_ref, b_ref, *refs):
    o_ref, both_ref = refs[-2:]
    step = pl.program_id(0)
    rows = x_ref.shape[0]
    slots = b_ref.shape[1]

    @pl.when(step == 0)
    def _():
        high, low = split(x_ref[...])
        both_ref[:rows] = high
        both_ref[rows:] = low

    for q in range(pair):
        r = at_ref[step] * pair + q
        total = jnp.zeros((rows, LANES), jnp.float32)
        for s in range(0, slots, 2):
            picks = [pl.ds(pl.multiple_of(cols_ref[r, s + h] * LANES, LANES), LANES) for h in range(2)]
            values = jnp.concatenate([both_ref[:, at] for at in picks], axis=1)
            bh, bl = split(jnp.concatenate([b_ref[q, s + h] for h in range(2)], axis=1))
            first = dot_nt(values, bh)
            total = total + first[:rows] + first[rows:] + dot_nt(values[:rows], bl)
        o_ref[:, q * LANES : (q + 1) * LANES] = total


def coupling(extended, local_cols, blocks, order, previous):
    rows = extended.shape[0]
    count, slots, size, _ = blocks.shape
    pair = 2
    in_specs = [
        pl.BlockSpec(extended.shape, lambda n, c, at: (0, 0)),
        pl.BlockSpec((pair, slots, size, size), lambda n, c, at: (at[n], 0, 0, 0)),
    ]
    args = [extended, blocks]
    if previous is not None:
        in_specs.append(pl.BlockSpec(memory_space=pl.ANY))
        args.append(previous)
    return pl.pallas_call(
        functools.partial(coupling_kernel, pair),
        out_shape=jax.ShapeDtypeStruct((rows, count * size), jnp.float32),
        grid_spec=pltpu.PrefetchScalarGridSpec(
            num_scalar_prefetch=2,
            grid=(len(order),),
            in_specs=in_specs,
            out_specs=pl.BlockSpec((rows, pair * size), lambda n, c, at: (0, at[n])),
            scratch_shapes=[pltpu.VMEM((2 * rows, extended.shape[1]), jnp.bfloat16)],
        ),
        input_output_aliases={4: 0} if previous is not None else {},
        compiler_params=pltpu.CompilerParams(vmem_limit_bytes=32 << 20),
        cost_estimate=pl.CostEstimate(
            flops=6 * rows * slots * size * size * pair * len(order), transcendentals=0,
            bytes_accessed=4 * slots * size * size * pair * len(order),
        ),
        name="coupling",
    )(local_cols, jnp.asarray(order, jnp.int32), *args)


def swapped(value, earlier):
    if earlier:
        value, earlier[-1] = lax.optimization_barrier((value, earlier[-1]))
    return lax.all_to_all(value, "fourier", split_axis=0, concat_axis=0, tiled=True)


def per_device(velocity, metrics, lumped_mass, element_ops, boundary_map, block_cols, schur_blocks):
    modes, elems = velocity.shape[1], velocity.shape[3]
    groups = lax.axis_size("fourier")
    part = lax.axis_index("fourier")
    slab = lax.axis_index("mer")
    slabs = lax.axis_size("mer")
    block_rows, block_size = schur_blocks.shape[0], schur_blocks.shape[2]
    owned_count = block_rows * block_size
    tiles = groups // ORDER
    chunks = elems // (tiles * LANES)

    v2 = velocity.reshape(3 * modes * NP, elems)
    v3 = velocity.reshape(3 * modes, NP, elems)
    mass = lumped_mass.reshape(ORDER, ORDER, elems)
    wave = jnp.asarray(spectral_tables(K)[3], jnp.float32)
    local_wave = lax.dynamic_slice_in_dim(wave, part * modes, modes)
    helm = 1.0 + 4.0 * (local_wave / (K / 2)) ** 2
    helm = jnp.broadcast_to(helm[:, None], (modes, LANES))
    order = np.argsort(np.argsort(kept))
    ids = jnp.stack([boundary_map[:, n] for n in order], axis=1) - slab * owned_count
    ids = ids.reshape(chunks, tiles, LANES, PERIM).transpose(0, 1, 3, 2).reshape(chunks, -1)
    ids = jnp.broadcast_to(ids[:, :, None], ids.shape + (LANES,))
    width = -(-(owned_count + block_size) // ASSEMBLED) * ASSEMBLED

    arrived = []
    for chunk in range(chunks):
        arrived.append(swapped(pack(v2, chunk, tiles, modes, groups), arrived))
    projected, order = [], []
    for chunk in range(chunks):
        first = (chunk * tiles + part // ORDER) * LANES + (part % ORDER) * SUB
        local_metrics = lax.dynamic_slice_in_dim(metrics, first, SUB, 2).reshape(4 * ORDER, LANES)
        counts = (3,) if chunk + 1 < chunks else (2, 1)
        pieces = physics(arrived[chunk].reshape(K, 3 * COLS), part % ORDER, local_metrics, counts)
        projected.append([piece.reshape(groups, modes, piece.shape[1]) for piece in pieces])
        order = [swapped(projected[chunk][0], order)]
        projected[chunk][0] = order[0]

    out, sums = None, None
    for chunk in range(chunks):
        values, first = [], 0
        if chunk + 1 == chunks:
            last = projected[chunk]
            if sums is not None:
                last[1], sums = lax.optimization_barrier((last[1], sums))
            last[1] = swapped(last[1], last[:1])
        for back in projected[chunk]:
            out, high, low = element_stage(
                v3, back, element_ops, mass, helm, out, chunk, tiles, modes, first
            )
            values.append((high, low))
            first += back.shape[2] // COLS
        sums = assemble(values, ids[chunk], sums, width)

    reach = HB * block_size
    up = [(i, i + 1) for i in range(slabs - 1)]
    down = [(i + 1, i) for i in range(slabs - 1)]
    from_below = lax.ppermute(sums[:, owned_count - reach : owned_count + block_size], "mer", up)
    from_above = lax.ppermute(sums[:, :reach], "mer", down)
    start = sums[:, :block_size] + from_below[:, reach:]
    after = from_above[:, :block_size] + sums[:, owned_count : owned_count + block_size]
    extended = jnp.concatenate(
        [from_below[:, :reach], start, sums[:, block_size:owned_count], after, from_above[:, block_size:]], axis=1
    )
    local_cols = block_cols - slab * block_rows
    pairs = block_rows // 2
    boundary_out = coupling(sums, local_cols, schur_blocks, range(2, pairs - 1), None)
    boundary_out = coupling(extended, local_cols + HB, schur_blocks, (0, 1, pairs - 1), boundary_out)
    return (out.reshape(velocity.shape), boundary_out.reshape(3, modes, owned_count))


def solution(mesh):
    in_specs = (
        P(None, "fourier", None, "mer"),
        P(None, None, "mer"),
        P(None, "mer"),
        P(None, None, "mer"),
        P("mer", None),
        P("mer", None),
        P("mer", None, None, None),
    )
    out_specs = (P(None, "fourier", None, "mer"), P(None, "fourier", "mer"))
    return jax.shard_map(
        per_device, mesh=mesh, in_specs=in_specs, out_specs=out_specs, check_vma=False
    )
```

```python
import functools

import jax
import jax.numpy as jnp
import numpy as np
from jax import lax
from jax.experimental import pallas as pl
from jax.experimental.pallas import tpu as pltpu
from jax.sharding import PartitionSpec as P

K = 256
HB = 2
NP = 64
ORDER = 8
LANES = 128
SUB = LANES // ORDER
WIDE = 256
COLS = NP * SUB
PERIM = 28
VMEM_LIMIT = 61 << 20
ASSEMBLED = 512


gauss_nodes = [
    -1.0,
    -0.8717401485096066,
    -0.5917001814331423,
    -0.2092992179024789,
    0.2092992179024789,
    0.5917001814331423,
    0.8717401485096066,
    1.0,
]
wave_scale = 1.0 / 32.0


def node_matrix():
    nodes = np.array(gauss_nodes)
    count = nodes.shape[0]
    barycentric = np.array(
        [1.0 / np.prod([nodes[i] - nodes[k] for k in range(count) if k != i]) for i in range(count)]
    )
    matrix = np.zeros((count, count))
    for i in range(count):
        for j in range(count):
            if i != j:
                matrix[i, j] = barycentric[j] / barycentric[i] / (nodes[i] - nodes[j])
        matrix[i, i] = -np.sum(matrix[i])
    return matrix


def spectral_tables(modes):
    planes = 3 * modes // 2
    index = np.arange(modes)
    wave = np.where(index == modes - 1, modes // 2, (index + 1) // 2)
    is_sine = (index % 2 == 0) & (index > 0) & (index < modes - 1)
    theta = 2.0 * np.pi * np.arange(planes) / planes
    angle = theta[:, None] * wave[None, :]
    basis = np.where(is_sine[None, :], np.sin(angle), np.cos(angle))
    deriv = wave_scale * wave[None, :] * np.where(is_sine[None, :], np.cos(angle), -np.sin(angle))
    weight = np.where(index == 0, 1.0, 2.0) / planes
    back = (basis * weight[None, :]).T
    return (basis, deriv, back, wave)


def halves(table):
    table = np.asarray(table, np.float32)
    high = table.astype(jnp.bfloat16)
    low = (table - high.astype(np.float32)).astype(jnp.bfloat16)
    return jnp.asarray(high), jnp.asarray(low)


def split(value):
    high = value.astype(jnp.bfloat16)
    low = (value - high.astype(jnp.float32)).astype(jnp.bfloat16)
    return high, low


def dot(left, right):
    return jnp.dot(left, right, preferred_element_type=jnp.float32)


def dot_nt(left, right):
    return lax.dot_general(left, right, (((1,), (1,)), ((), ())), preferred_element_type=jnp.float32)


def groups_picked(rows):
    lane = lax.broadcasted_iota(jnp.int32, rows[0].shape, 1)
    for step in (4, 2, 1):
        upper = (lane & (step * SUB)) != 0
        rows = [jnp.where(upper, rows[(i + step) % ORDER], rows[i]) for i in range(ORDER)]
    return [rows[-g % ORDER] for g in range(ORDER)]


def rolled(row, groups):
    shift = groups % ORDER * SUB
    return pltpu.roll(row, shift, 1) if shift else row


def sublane_groups_swapped(rows):
    rows = list(rows)
    line = lax.broadcasted_iota(jnp.int32, (ORDER, LANES), 0)
    for step in (4, 2, 1):
        lower = (line & step) == 0
        for i in range(ORDER):
            if i & step:
                continue
            top, bottom = rows[i], rows[i + step]
            rows[i] = jnp.where(lower, top, pltpu.roll(bottom, step, 0))
            rows[i + step] = jnp.where(lower, pltpu.roll(top, ORDER - step, 0), bottom)
    return rows


def partner_order(groups):
    return [0, 1] + sorted(range(2, groups), key=lambda s: (-bin(s >> 1).count("1"), s & 1, s))


def partners_swapped(rows, me):
    rows = list(rows)
    bit = 1
    while bit < len(rows):
        swap = (jnp.zeros(rows[0].shape, jnp.int32) + (me & bit)) != 0
        for i in range(len(rows)):
            if i & bit:
                continue
            top, bottom = rows[i], rows[i + bit]
            rows[i] = jnp.where(swap, bottom, top)
            rows[i + bit] = jnp.where(swap, top, bottom)
        bit *= 2
    return rows


def pack_kernel(modes, tiles, me_ref, v_ref, *o_refs):
    me = me_ref[0]
    for a in range(ORDER):
        pieces = []
        for t in range(tiles):
            lanes = slice(t * LANES, (t + 1) * LANES)
            bands = [
                sublane_groups_swapped([v_ref[u + k, a * ORDER : (a + 1) * ORDER, lanes] for k in range(ORDER)])
                for u in range(0, modes, ORDER)
            ]
            rows = [jnp.concatenate(band, axis=0) for band in zip(*bands)]
            pieces += groups_picked([rolled(row, b) for b, row in enumerate(rows)])
        pieces = partners_swapped(pieces, me)
        for o_ref, s in zip(o_refs, partner_order(len(o_refs))):
            o_ref[:, a * LANES : (a + 1) * LANES] = pieces[s]


def pack(v3, me, chunk, tiles, modes, groups):
    return pl.pallas_call(
        functools.partial(pack_kernel, modes, tiles),
        out_shape=[jax.ShapeDtypeStruct((modes, 3 * COLS), jnp.float32)] * groups,
        grid_spec=pltpu.PrefetchScalarGridSpec(
            num_scalar_prefetch=1,
            grid=(3,),
            in_specs=[pl.BlockSpec((modes, NP, tiles * LANES), lambda f, m: (f, 0, chunk))],
            out_specs=[pl.BlockSpec((modes, COLS), lambda f, m: (0, f))] * groups,
        ),
        compiler_params=pltpu.CompilerParams(vmem_limit_bytes=VMEM_LIMIT),
        cost_estimate=pl.CostEstimate(flops=0, transcendentals=0, bytes_accessed=8 * 3 * tiles * modes * NP * LANES),
        name="pack",
    )(me, v3)


def permuted(pieces):
    groups = len(pieces)
    return [
        lax.ppermute(piece, "fourier", [(i, i ^ s) for i in range(groups)]) if s else piece
        for s, piece in zip(partner_order(groups), pieces)
    ]


def physics_kernel(planes, even, odd, groups, counts, me_ref, fh_ref, fl_ref, wh_ref, wl_ref, bh_ref, bl_ref, m_ref,
                   *refs):
    pieces, outs = refs[:groups], refs[groups : groups + len(counts)]
    x_ref, y_ref, p_ref, z_ref, s_ref, ah_ref, al_ref, in_sem, out_sem = refs[groups + len(counts) :]
    modes = K // groups
    width = 3 * COLS

    arriving = []
    for n, partner in enumerate(partner_order(groups)):
        rows = pl.ds(pl.multiple_of((me_ref[0] ^ partner) * modes, modes), modes)
        arriving.append(pltpu.make_async_copy(pieces[n], x_ref.at[rows, :], in_sem.at[n]))
        arriving[n].start()
    for copy in arriving:
        copy.wait()

    def forward(tile, carry):
        cols = pl.ds(pl.multiple_of(tile * WIDE, WIDE), WIDE)
        xh, xl = split(x_ref[:, cols])
        fh = fh_ref[...]
        both = dot(fh, xh) + dot(fl_ref[...], xh) + dot(fh, xl)
        values = both[:planes]
        p_ref[:, cols] = values
        z_ref[:, cols] = both[planes:]
        ph, plo = split(values)
        wh = wh_ref[...]
        s_ref[:, cols] = dot(ph, wh) + dot(plo, wh) + dot(ph, wl_ref[...])
        return carry

    lax.fori_loop(0, width // WIDE, forward, 0)

    step = 16

    def products(tile, carry):
        rows = pl.ds(pl.multiple_of(tile * step, step), step)

        def piece(ref, f, a):
            start = f * COLS + a * LANES
            return ref[rows, start : start + LANES]

        speed_r, speed_s, speed_z = [], [], []
        for a in range(ORDER):
            p0, p1, p2 = (piece(p_ref, f, a) for f in range(3))
            m0, m1, m2, m3 = (m_ref[ORDER * q + a : ORDER * q + a + 1, :] for q in range(4))
            speed_r.append(p0 * m0 + p1 * m1)
            speed_s.append(p0 * m2 + p1 * m3)
            speed_z.append(p2)
        for f in range(3):
            values = [piece(p_ref, f, a) for a in range(ORDER)]
            total = [values[j] + values[7 - j] for j in range(4)]
            diff = [values[j] - values[7 - j] for j in range(4)]
            for i in range(4):
                e = even[i][0] * total[0]
                o = odd[i][0] * diff[0]
                for j in range(1, 4):
                    e = e + even[i][j] * total[j]
                    o = o + odd[i][j] * diff[j]
                for a, along in ((i, o + e), (7 - i, o - e)):
                    out = speed_r[a] * along + speed_s[a] * piece(s_ref, f, a) + speed_z[a] * piece(z_ref, f, a)
                    high, low = split(out)
                    start = f * COLS + a * LANES
                    ah_ref[rows, start : start + LANES] = high
                    al_ref[rows, start : start + LANES] = low
        return carry

    lax.fori_loop(0, planes // step, products, 0)

    def backward(tile, carry):
        cols = pl.ds(pl.multiple_of(tile * WIDE, WIDE), WIDE)
        ah = ah_ref[:, cols]
        bh = bh_ref[...]
        y_ref[:, cols] = dot(bh, ah) + dot(bl_ref[...], ah) + dot(bh, al_ref[:, cols])
        return carry

    start, leaving = 0, []
    for n, count in enumerate(counts):
        stop = start + count * COLS
        lax.fori_loop(start // WIDE, stop // WIDE, backward, 0)
        leaving.append(pltpu.make_async_copy(y_ref.at[:, start:stop], outs[n], out_sem.at[n]))
        leaving[-1].start()
        start = stop
    for copy in leaving:
        copy.wait()


def physics(received, me, turn, metrics, counts):
    groups = len(received)
    basis, deriv, back, _ = spectral_tables(K)
    planes = basis.shape[0]
    width = 3 * COLS
    fh, fl = halves(np.concatenate([basis, deriv], axis=0))
    bh, bl = halves(-back)
    matrix = node_matrix()
    metrics = jnp.roll(metrics, turn * SUB, 1)
    wh, wl = (jnp.roll(table, (turn, turn), (0, 1)) for table in halves(matrix.T))
    spread = [jnp.eye(n, dtype=jnp.bfloat16) for n in (WIDE // LANES, SUB)]
    wh, wl = (
        jnp.einsum("xy,bc,ef->xbeycf", spread[0], table, spread[1]).reshape(WIDE, WIDE) for table in (wh, wl)
    )
    flipped = matrix[:, ::-1]
    even = ((matrix + flipped) / 2)[:4, :4].astype(np.float32).tolist()
    odd = ((matrix - flipped) / 2)[:4, :4].astype(np.float32).tolist()
    return pl.pallas_call(
        functools.partial(physics_kernel, planes, even, odd, groups, counts),
        out_shape=[jax.ShapeDtypeStruct((K, count * COLS), jnp.float32) for count in counts],
        in_specs=[pl.BlockSpec(memory_space=pltpu.SMEM)]
        + [pl.BlockSpec(memory_space=pltpu.VMEM)] * 7
        + [pl.BlockSpec(memory_space=pl.ANY)] * groups,
        out_specs=[pl.BlockSpec(memory_space=pl.ANY)] * len(counts),
        scratch_shapes=[pltpu.VMEM((K, width), jnp.float32)] * 2
        + [pltpu.VMEM((planes, width), jnp.float32)] * 3
        + [pltpu.VMEM((planes, width), jnp.bfloat16)] * 2
        + [pltpu.SemaphoreType.DMA((groups,)), pltpu.SemaphoreType.DMA((len(counts),))],
        compiler_params=pltpu.CompilerParams(vmem_limit_bytes=VMEM_LIMIT),
        cost_estimate=pl.CostEstimate(
            flops=6 * planes * width * (3 * K + WIDE), transcendentals=0, bytes_accessed=8 * K * width
        ),
        name="physics",
    )(me, fh, fl, wh, wl, bh, bl, metrics, *received)


def element_kernel(modes, aliased, v_ref, r_ref, a_ref, mass_ref, helm_ref, *refs):
    o_ref, high_ref, low_ref, f_ref = refs[1:] if aliased else refs
    bands = modes // ORDER
    for a in range(ORDER):
        rows = groups_picked([r_ref[g, :, a * LANES : (a + 1) * LANES] for g in range(ORDER)])
        rows = [rolled(row, -b) for b, row in enumerate(rows)]
        for u in range(bands):
            own = sublane_groups_swapped([v_ref[ORDER * u + k, a * ORDER : (a + 1) * ORDER, :] for k in range(ORDER)])
            for b in range(ORDER):
                f_ref[ORDER * a + b, ORDER * u : ORDER * (u + 1), :] = own[b] + rows[b][ORDER * u : ORDER * (u + 1), :]

    def op_rows(a, carry):
        first = pl.multiple_of(a * ORDER, ORDER)
        sums = []
        for b in range(ORDER):
            weight = helm_ref[...] * mass_ref[a, b : b + 1, :]
            own = f_ref[first + b]
            sums.append([(weight * own)[ORDER * u : ORDER * (u + 1), :] for u in range(bands)])
        for j in range(NP):
            value = f_ref[j]
            for b in range(ORDER):
                weight = a_ref[first + b, j : j + 1, :]
                for u in range(bands):
                    sums[b][u] = sums[b][u] + weight * value[ORDER * u : ORDER * (u + 1), :]

        def keep(b, slot):
            at = pl.ds(pl.multiple_of(slot * LANES, LANES), LANES)
            high, low = split(jnp.concatenate(sums[b], axis=0))
            high_ref[:, at] = high
            low_ref[:, at] = low

        keep(0, 2 * a)
        keep(ORDER - 1, 2 * a + 1)

        @pl.when((a == 0) | (a == ORDER - 1))
        def _():
            for b in range(1, ORDER - 1):
                keep(b, 2 * ORDER + jnp.where(a == 0, 0, ORDER - 2) + b - 1)

        for u in range(bands):
            rows = sublane_groups_swapped([sums[b][u] for b in range(ORDER)])
            for k in range(ORDER):
                o_ref[ORDER * u + k, pl.ds(first, ORDER), :] = rows[k]
        return carry

    lax.fori_loop(0, ORDER, op_rows, 0)


kept = [8 * a + b for a in range(8) for b in (0, 7)] + [8 * a + b for a in (0, 7) for b in range(1, 7)]


def element_stage(v3, received, ops, mass, helm, previous, chunk, tiles, modes, first):
    count = received.shape[2] // COLS
    aliased = previous is not None
    in_specs = [
        pl.BlockSpec((modes, NP, LANES), lambda t, f: (first + f, 0, chunk * tiles + t)),
        pl.BlockSpec((ORDER, modes, COLS), lambda t, f: (t, 0, f)),
        pl.BlockSpec((NP, NP, LANES), lambda t, f: (0, 0, chunk * tiles + t)),
        pl.BlockSpec((ORDER, ORDER, LANES), lambda t, f: (0, 0, chunk * tiles + t)),
        pl.BlockSpec((modes, LANES), lambda t, f: (0, 0)),
    ]
    args = [v3, received, ops, mass, helm]
    if aliased:
        in_specs.append(pl.BlockSpec(memory_space=pl.ANY))
        args.append(previous)
    values = jax.ShapeDtypeStruct((count * modes, tiles * PERIM * LANES), jnp.bfloat16)
    values_spec = pl.BlockSpec((modes, PERIM * LANES), lambda t, f: (f, t))
    return pl.pallas_call(
        functools.partial(element_kernel, modes, aliased),
        out_shape=(jax.ShapeDtypeStruct(v3.shape, jnp.float32), values, values),
        grid=(tiles, count),
        in_specs=in_specs,
        out_specs=(
            pl.BlockSpec((modes, NP, LANES), lambda t, f: (first + f, 0, chunk * tiles + t)),
            values_spec,
            values_spec,
        ),
        scratch_shapes=[pltpu.VMEM((NP, modes, LANES), jnp.float32)],
        input_output_aliases={5: 0} if aliased else {},
        compiler_params=pltpu.CompilerParams(vmem_limit_bytes=VMEM_LIMIT),
        cost_estimate=pl.CostEstimate(
            flops=2 * count * tiles * modes * NP * NP * LANES, transcendentals=0,
            bytes_accessed=4 * 4 * count * tiles * modes * NP * LANES,
        ),
        name="element",
    )(*args)


def assemble_kernel(parts, block, *refs):
    ids_ref, o_ref = refs[2 * parts], refs[-1]
    rows, depth = o_ref.shape[0], refs[0].shape[1]
    wanted = lax.broadcasted_iota(jnp.int32, (WIDE, LANES), 1) + pl.program_id(0) * block
    total = jnp.zeros((2 * rows, block), jnp.float32)
    for start in range(0, depth, WIDE):
        ids = ids_ref[start : start + WIDE, :] - wanted
        hot = [jnp.where(ids == LANES * h, 1.0, 0.0).astype(jnp.bfloat16) for h in range(block // LANES)]
        values = jnp.concatenate([ref[:, start : start + WIDE] for ref in refs[: 2 * parts]], axis=0)
        total = total + dot(values, jnp.concatenate(hot, axis=1))
    total = total[:rows] + total[rows:]
    o_ref[...] = total if len(refs) == 2 * parts + 2 else refs[-2][...] + total


def assemble(values, ids, before, width, block=ASSEMBLED):
    highs, lows = zip(*values)
    rows, depth = sum(high.shape[0] for high in highs), highs[0].shape[1]
    in_specs = [pl.BlockSpec(memory_space=pltpu.VMEM)] * (2 * len(values) + 1)
    args = [*highs, *lows, ids]
    if before is not None:
        in_specs.append(pl.BlockSpec((rows, block), lambda n: (0, n)))
        args.append(before)
    return pl.pallas_call(
        functools.partial(assemble_kernel, len(values), block),
        out_shape=jax.ShapeDtypeStruct((rows, width), jnp.float32),
        grid=(width // block,),
        in_specs=in_specs,
        out_specs=pl.BlockSpec((rows, block), lambda n: (0, n)),
        compiler_params=pltpu.CompilerParams(vmem_limit_bytes=32 << 20),
        cost_estimate=pl.CostEstimate(
            flops=4 * rows * depth * width, transcendentals=0, bytes_accessed=4 * (2 * rows + LANES) * depth
        ),
        name="assemble",
    )(*args)


def coupling_kernel(pair, cols_ref, at_ref, x_ref, b_ref, *refs):
    o_ref, both_ref = refs[-2:]
    step = pl.program_id(0)
    rows = x_ref.shape[0]
    slots = b_ref.shape[1]

    @pl.when(step == 0)
    def _():
        high, low = split(x_ref[...])
        both_ref[:rows] = high
        both_ref[rows:] = low

    for q in range(pair):
        r = at_ref[step] * pair + q
        total = jnp.zeros((rows, LANES), jnp.float32)
        for s in range(0, slots, 2):
            picks = [pl.ds(pl.multiple_of(cols_ref[r, s + h] * LANES, LANES), LANES) for h in range(2)]
            values = jnp.concatenate([both_ref[:, at] for at in picks], axis=1)
            bh, bl = split(jnp.concatenate([b_ref[q, s + h] for h in range(2)], axis=1))
            first = dot_nt(values, bh)
            total = total + first[:rows] + first[rows:] + dot_nt(values[:rows], bl)
        o_ref[:, q * LANES : (q + 1) * LANES] = total


def coupling(extended, local_cols, blocks, order, previous):
    rows = extended.shape[0]
    count, slots, size, _ = blocks.shape
    pair = 2
    in_specs = [
        pl.BlockSpec(extended.shape, lambda n, c, at: (0, 0)),
        pl.BlockSpec((pair, slots, size, size), lambda n, c, at: (at[n], 0, 0, 0)),
    ]
    args = [extended, blocks]
    if previous is not None:
        in_specs.append(pl.BlockSpec(memory_space=pl.ANY))
        args.append(previous)
    return pl.pallas_call(
        functools.partial(coupling_kernel, pair),
        out_shape=jax.ShapeDtypeStruct((rows, count * size), jnp.float32),
        grid_spec=pltpu.PrefetchScalarGridSpec(
            num_scalar_prefetch=2,
            grid=(len(order),),
            in_specs=in_specs,
            out_specs=pl.BlockSpec((rows, pair * size), lambda n, c, at: (0, at[n])),
            scratch_shapes=[pltpu.VMEM((2 * rows, extended.shape[1]), jnp.bfloat16)],
        ),
        input_output_aliases={4: 0} if previous is not None else {},
        compiler_params=pltpu.CompilerParams(vmem_limit_bytes=32 << 20),
        cost_estimate=pl.CostEstimate(
            flops=6 * rows * slots * size * size * pair * len(order), transcendentals=0,
            bytes_accessed=4 * slots * size * size * pair * len(order),
        ),
        name="coupling",
    )(local_cols, jnp.asarray(order, jnp.int32), *args)


def swapped(value, earlier):
    if earlier:
        value, earlier[-1] = lax.optimization_barrier((value, earlier[-1]))
    return lax.all_to_all(value, "fourier", split_axis=0, concat_axis=0, tiled=True)


def per_device(velocity, metrics, lumped_mass, element_ops, boundary_map, block_cols, schur_blocks):
    modes, elems = velocity.shape[1], velocity.shape[3]
    groups = lax.axis_size("fourier")
    part = lax.axis_index("fourier")
    slab = lax.axis_index("mer")
    slabs = lax.axis_size("mer")
    block_rows, block_size = schur_blocks.shape[0], schur_blocks.shape[2]
    owned_count = block_rows * block_size
    tiles = groups // ORDER
    chunks = elems // (tiles * LANES)

    v3 = velocity.reshape(3 * modes, NP, elems)
    mass = lumped_mass.reshape(ORDER, ORDER, elems)
    wave = jnp.asarray(spectral_tables(K)[3], jnp.float32)
    local_wave = lax.dynamic_slice_in_dim(wave, part * modes, modes)
    helm = 1.0 + 4.0 * (local_wave / (K / 2)) ** 2
    helm = jnp.broadcast_to(helm[:, None], (modes, LANES))
    order = np.argsort(np.argsort(kept))
    ids = jnp.stack([boundary_map[:, n] for n in order], axis=1) - slab * owned_count
    ids = ids.reshape(chunks, tiles, LANES, PERIM).transpose(0, 1, 3, 2).reshape(chunks, -1)
    ids = jnp.broadcast_to(ids[:, :, None], ids.shape + (LANES,))
    width = -(-(owned_count + block_size) // ASSEMBLED) * ASSEMBLED

    me = jnp.reshape(part, (1,))
    arrived, source = [], v3
    for chunk in range(chunks):
        got = permuted(pack(source, me, chunk, tiles, modes, groups))
        if chunk + 1 < chunks:
            source, got[1] = lax.optimization_barrier((v3, got[1]))
        arrived.append(got)

    for now, later in zip(arrived, arrived[1:]):
        now[0], later[1] = lax.optimization_barrier((now[0], later[1]))

    projected, order = [], []
    for chunk in range(chunks):
        first = (chunk * tiles + part // ORDER) * LANES + (part % ORDER) * SUB
        local_metrics = lax.dynamic_slice_in_dim(metrics, first, SUB, 2).reshape(4 * ORDER, LANES)
        counts = (3,) if chunk + 1 < chunks else (2, 1)
        pieces = physics(arrived[chunk], me, part % ORDER, local_metrics, counts)
        projected.append([piece.reshape(groups, modes, piece.shape[1]) for piece in pieces])
        if chunk + 1 < chunks:
            both = (projected[chunk][0], arrived[chunk + 1])
            projected[chunk][0], arrived[chunk + 1] = lax.optimization_barrier(both)
        order = [swapped(projected[chunk][0], order)]
        projected[chunk][0] = order[0]

    out, sums = None, None
    for chunk in range(chunks):
        values, first = [], 0
        if chunk + 1 == chunks:
            last = projected[chunk]
            if sums is not None:
                last[1], sums = lax.optimization_barrier((last[1], sums))
            last[1] = swapped(last[1], last[:1])
        for back in projected[chunk]:
            out, high, low = element_stage(
                v3, back, element_ops, mass, helm, out, chunk, tiles, modes, first
            )
            values.append((high, low))
            first += back.shape[2] // COLS
        sums = assemble(values, ids[chunk], sums, width)

    reach = HB * block_size
    up = [(i, i + 1) for i in range(slabs - 1)]
    down = [(i + 1, i) for i in range(slabs - 1)]
    from_below = lax.ppermute(sums[:, owned_count - reach : owned_count + block_size], "mer", up)
    from_above = lax.ppermute(sums[:, :reach], "mer", down)
    start = sums[:, :block_size] + from_below[:, reach:]
    after = from_above[:, :block_size] + sums[:, owned_count : owned_count + block_size]
    extended = jnp.concatenate(
        [from_below[:, :reach], start, sums[:, block_size:owned_count], after, from_above[:, block_size:]], axis=1
    )
    local_cols = block_cols - slab * block_rows
    pairs = block_rows // 2
    boundary_out = coupling(sums, local_cols, schur_blocks, range(2, pairs - 1), None)
    boundary_out = coupling(extended, local_cols + HB, schur_blocks, (0, 1, pairs - 1), boundary_out)
    return (out.reshape(velocity.shape), boundary_out.reshape(3, modes, owned_count))


def solution(mesh):
    in_specs = (
        P(None, "fourier", None, "mer"),
        P(None, None, "mer"),
        P(None, "mer"),
        P(None, None, "mer"),
        P("mer", None),
        P("mer", None),
        P("mer", None, None, None),
    )
    out_specs = (P(None, "fourier", None, "mer"), P(None, "fourier", "mer"))
    return jax.shard_map(
        per_device, mesh=mesh, in_specs=in_specs, out_specs=out_specs, check_vma=False
    )
```

```python
import functools

import jax
import jax.numpy as jnp
import numpy as np
from jax import lax
from jax.experimental import pallas as pl
from jax.experimental.pallas import tpu as pltpu
from jax.sharding import PartitionSpec as P

K = 256
HB = 2
NP = 64
ORDER = 8
LANES = 128
SUB = LANES // ORDER
WIDE = 256
COLS = NP * SUB
PERIM = 28
VMEM_LIMIT = 61 << 20
ASSEMBLED = 512


gauss_nodes = [
    -1.0,
    -0.8717401485096066,
    -0.5917001814331423,
    -0.2092992179024789,
    0.2092992179024789,
    0.5917001814331423,
    0.8717401485096066,
    1.0,
]
wave_scale = 1.0 / 32.0


def node_matrix():
    nodes = np.array(gauss_nodes)
    count = nodes.shape[0]
    barycentric = np.array(
        [1.0 / np.prod([nodes[i] - nodes[k] for k in range(count) if k != i]) for i in range(count)]
    )
    matrix = np.zeros((count, count))
    for i in range(count):
        for j in range(count):
            if i != j:
                matrix[i, j] = barycentric[j] / barycentric[i] / (nodes[i] - nodes[j])
        matrix[i, i] = -np.sum(matrix[i])
    return matrix


def spectral_tables(modes):
    planes = 3 * modes // 2
    index = np.arange(modes)
    wave = np.where(index == modes - 1, modes // 2, (index + 1) // 2)
    is_sine = (index % 2 == 0) & (index > 0) & (index < modes - 1)
    theta = 2.0 * np.pi * np.arange(planes) / planes
    angle = theta[:, None] * wave[None, :]
    basis = np.where(is_sine[None, :], np.sin(angle), np.cos(angle))
    deriv = wave_scale * wave[None, :] * np.where(is_sine[None, :], np.cos(angle), -np.sin(angle))
    weight = np.where(index == 0, 1.0, 2.0) / planes
    back = (basis * weight[None, :]).T
    return (basis, deriv, back, wave)


def halves(table):
    table = np.asarray(table, np.float32)
    high = table.astype(jnp.bfloat16)
    low = (table - high.astype(np.float32)).astype(jnp.bfloat16)
    return jnp.asarray(high), jnp.asarray(low)


def split(value):
    high = value.astype(jnp.bfloat16)
    low = (value - high.astype(jnp.float32)).astype(jnp.bfloat16)
    return high, low


def dot(left, right):
    return jnp.dot(left, right, preferred_element_type=jnp.float32)


def dot_nt(left, right):
    return lax.dot_general(left, right, (((1,), (1,)), ((), ())), preferred_element_type=jnp.float32)


def groups_picked(rows):
    lane = lax.broadcasted_iota(jnp.int32, rows[0].shape, 1)
    for step in (4, 2, 1):
        upper = (lane & (step * SUB)) != 0
        rows = [jnp.where(upper, rows[(i + step) % ORDER], rows[i]) for i in range(ORDER)]
    return [rows[-g % ORDER] for g in range(ORDER)]


def rolled(row, groups):
    shift = groups % ORDER * SUB
    return pltpu.roll(row, shift, 1) if shift else row


def sublane_groups_swapped(rows):
    rows = list(rows)
    line = lax.broadcasted_iota(jnp.int32, (ORDER, LANES), 0)
    for step in (4, 2, 1):
        lower = (line & step) == 0
        for i in range(ORDER):
            if i & step:
                continue
            top, bottom = rows[i], rows[i + step]
            rows[i] = jnp.where(lower, top, pltpu.roll(bottom, step, 0))
            rows[i + step] = jnp.where(lower, pltpu.roll(top, ORDER - step, 0), bottom)
    return rows


def partner_order(groups):
    return [0, 1] + sorted(range(2, groups), key=lambda s: (-bin(s >> 1).count("1"), s & 1, s))


def partners_swapped(rows, me):
    rows = list(rows)
    bit = 1
    while bit < len(rows):
        swap = (jnp.zeros(rows[0].shape, jnp.int32) + (me & bit)) != 0
        for i in range(len(rows)):
            if i & bit:
                continue
            top, bottom = rows[i], rows[i + bit]
            rows[i] = jnp.where(swap, bottom, top)
            rows[i + bit] = jnp.where(swap, top, bottom)
        bit *= 2
    return rows


def pack_kernel(modes, tiles, me_ref, v_ref, *o_refs):
    me = me_ref[0]
    for a in range(ORDER):
        pieces = []
        for t in range(tiles):
            lanes = slice(t * LANES, (t + 1) * LANES)
            bands = [
                sublane_groups_swapped([v_ref[u + k, a * ORDER : (a + 1) * ORDER, lanes] for k in range(ORDER)])
                for u in range(0, modes, ORDER)
            ]
            rows = [jnp.concatenate(band, axis=0) for band in zip(*bands)]
            pieces += groups_picked([rolled(row, b) for b, row in enumerate(rows)])
        pieces = partners_swapped(pieces, me)
        for o_ref, s in zip(o_refs, partner_order(len(o_refs))):
            o_ref[:, a * LANES : (a + 1) * LANES] = pieces[s]


def pack(v3, me, chunk, tiles, modes, groups):
    return pl.pallas_call(
        functools.partial(pack_kernel, modes, tiles),
        out_shape=[jax.ShapeDtypeStruct((modes, 3 * COLS), jnp.float32)] * groups,
        grid_spec=pltpu.PrefetchScalarGridSpec(
            num_scalar_prefetch=1,
            grid=(3,),
            in_specs=[pl.BlockSpec((modes, NP, tiles * LANES), lambda f, m: (f, 0, chunk))],
            out_specs=[pl.BlockSpec((modes, COLS), lambda f, m: (0, f))] * groups,
        ),
        compiler_params=pltpu.CompilerParams(vmem_limit_bytes=VMEM_LIMIT),
        cost_estimate=pl.CostEstimate(flops=0, transcendentals=0, bytes_accessed=8 * 3 * tiles * modes * NP * LANES),
        name="pack",
    )(me, v3)


def permuted(pieces):
    groups = len(pieces)
    return [
        lax.ppermute(piece, "fourier", [(i, i ^ s) for i in range(groups)]) if s else piece
        for s, piece in zip(partner_order(groups), pieces)
    ]


def physics_kernel(planes, even, odd, groups, counts, me_ref, fh_ref, fl_ref, wh_ref, wl_ref, bh_ref, bl_ref, m_ref,
                   *refs):
    pieces, outs = refs[:groups], refs[groups : groups + len(counts)]
    x_ref, y_ref, p_ref, z_ref, s_ref, ah_ref, al_ref, in_sem, out_sem = refs[groups + len(counts) :]
    modes = K // groups
    width = 3 * COLS

    arriving = []
    for n, partner in enumerate(partner_order(groups)):
        rows = pl.ds(pl.multiple_of((me_ref[0] ^ partner) * modes, modes), modes)
        arriving.append(pltpu.make_async_copy(pieces[n], x_ref.at[rows, :], in_sem.at[n]))
        arriving[n].start()
    for copy in arriving:
        copy.wait()

    def forward(tile, carry):
        cols = pl.ds(pl.multiple_of(tile * WIDE, WIDE), WIDE)
        xh, xl = split(x_ref[:, cols])
        fh = fh_ref[...]
        both = dot(fh, xh) + dot(fl_ref[...], xh) + dot(fh, xl)
        values = both[:planes]
        p_ref[:, cols] = values
        z_ref[:, cols] = both[planes:]
        ph, plo = split(values)
        wh = wh_ref[...]
        s_ref[:, cols] = dot(ph, wh) + dot(plo, wh) + dot(ph, wl_ref[...])
        return carry

    lax.fori_loop(0, width // WIDE, forward, 0)

    step = 16

    def products(tile, carry):
        rows = pl.ds(pl.multiple_of(tile * step, step), step)

        def piece(ref, f, a):
            start = f * COLS + a * LANES
            return ref[rows, start : start + LANES]

        speed_r, speed_s, speed_z = [], [], []
        for a in range(ORDER):
            p0, p1, p2 = (piece(p_ref, f, a) for f in range(3))
            m0, m1, m2, m3 = (m_ref[ORDER * q + a : ORDER * q + a + 1, :] for q in range(4))
            speed_r.append(p0 * m0 + p1 * m1)
            speed_s.append(p0 * m2 + p1 * m3)
            speed_z.append(p2)
        for f in range(3):
            values = [piece(p_ref, f, a) for a in range(ORDER)]
            total = [values[j] + values[7 - j] for j in range(4)]
            diff = [values[j] - values[7 - j] for j in range(4)]
            for i in range(4):
                e = even[i][0] * total[0]
                o = odd[i][0] * diff[0]
                for j in range(1, 4):
                    e = e + even[i][j] * total[j]
                    o = o + odd[i][j] * diff[j]
                for a, along in ((i, o + e), (7 - i, o - e)):
                    out = speed_r[a] * along + speed_s[a] * piece(s_ref, f, a) + speed_z[a] * piece(z_ref, f, a)
                    high, low = split(out)
                    start = f * COLS + a * LANES
                    ah_ref[rows, start : start + LANES] = high
                    al_ref[rows, start : start + LANES] = low
        return carry

    lax.fori_loop(0, planes // step, products, 0)

    def backward(tile, carry):
        cols = pl.ds(pl.multiple_of(tile * WIDE, WIDE), WIDE)
        ah = ah_ref[:, cols]
        bh = bh_ref[...]
        y_ref[:, cols] = dot(bh, ah) + dot(bl_ref[...], ah) + dot(bh, al_ref[:, cols])
        return carry

    start, leaving = 0, []
    for n, count in enumerate(counts):
        stop = start + count * COLS
        lax.fori_loop(start // WIDE, stop // WIDE, backward, 0)
        leaving.append(pltpu.make_async_copy(y_ref.at[:, start:stop], outs[n], out_sem.at[n]))
        leaving[-1].start()
        start = stop
    for copy in leaving:
        copy.wait()


def physics(received, me, turn, metrics, counts):
    groups = len(received)
    basis, deriv, back, _ = spectral_tables(K)
    planes = basis.shape[0]
    width = 3 * COLS
    fh, fl = halves(np.concatenate([basis, deriv], axis=0))
    bh, bl = halves(-back)
    matrix = node_matrix()
    metrics = jnp.roll(metrics, turn * SUB, 1)
    wh, wl = (jnp.roll(table, (turn, turn), (0, 1)) for table in halves(matrix.T))
    spread = [jnp.eye(n, dtype=jnp.bfloat16) for n in (WIDE // LANES, SUB)]
    wh, wl = (
        jnp.einsum("xy,bc,ef->xbeycf", spread[0], table, spread[1]).reshape(WIDE, WIDE) for table in (wh, wl)
    )
    flipped = matrix[:, ::-1]
    even = ((matrix + flipped) / 2)[:4, :4].astype(np.float32).tolist()
    odd = ((matrix - flipped) / 2)[:4, :4].astype(np.float32).tolist()
    return pl.pallas_call(
        functools.partial(physics_kernel, planes, even, odd, groups, counts),
        out_shape=[jax.ShapeDtypeStruct((K, count * COLS), jnp.float32) for count in counts],
        in_specs=[pl.BlockSpec(memory_space=pltpu.SMEM)]
        + [pl.BlockSpec(memory_space=pltpu.VMEM)] * 7
        + [pl.BlockSpec(memory_space=pl.ANY)] * groups,
        out_specs=[pl.BlockSpec(memory_space=pl.ANY)] * len(counts),
        scratch_shapes=[pltpu.VMEM((K, width), jnp.float32)] * 2
        + [pltpu.VMEM((planes, width), jnp.float32)] * 3
        + [pltpu.VMEM((planes, width), jnp.bfloat16)] * 2
        + [pltpu.SemaphoreType.DMA((groups,)), pltpu.SemaphoreType.DMA((len(counts),))],
        compiler_params=pltpu.CompilerParams(vmem_limit_bytes=VMEM_LIMIT),
        cost_estimate=pl.CostEstimate(
            flops=6 * planes * width * (3 * K + WIDE), transcendentals=0, bytes_accessed=8 * K * width
        ),
        name="physics",
    )(me, fh, fl, wh, wl, bh, bl, metrics, *received)


def element_kernel(modes, aliased, v_ref, r_ref, a_ref, mass_ref, helm_ref, *refs):
    o_ref, high_ref, low_ref, f_ref = refs[1:] if aliased else refs
    bands = modes // ORDER
    for a in range(ORDER):
        rows = groups_picked([r_ref[g, :, a * LANES : (a + 1) * LANES] for g in range(ORDER)])
        rows = [rolled(row, -b) for b, row in enumerate(rows)]
        for u in range(bands):
            own = sublane_groups_swapped([v_ref[ORDER * u + k, a * ORDER : (a + 1) * ORDER, :] for k in range(ORDER)])
            for b in range(ORDER):
                f_ref[ORDER * a + b, ORDER * u : ORDER * (u + 1), :] = own[b] + rows[b][ORDER * u : ORDER * (u + 1), :]

    def op_rows(a, carry):
        first = pl.multiple_of(a * ORDER, ORDER)
        sums = []
        for b in range(ORDER):
            weight = helm_ref[...] * mass_ref[a, b : b + 1, :]
            own = f_ref[first + b]
            sums.append([(weight * own)[ORDER * u : ORDER * (u + 1), :] for u in range(bands)])
        for j in range(NP):
            value = f_ref[j]
            for b in range(ORDER):
                weight = a_ref[first + b, j : j + 1, :]
                for u in range(bands):
                    sums[b][u] = sums[b][u] + weight * value[ORDER * u : ORDER * (u + 1), :]

        def keep(b, slot):
            at = pl.ds(pl.multiple_of(slot * LANES, LANES), LANES)
            high, low = split(jnp.concatenate(sums[b], axis=0))
            high_ref[:, at] = high
            low_ref[:, at] = low

        keep(0, 2 * a)
        keep(ORDER - 1, 2 * a + 1)

        @pl.when((a == 0) | (a == ORDER - 1))
        def _():
            for b in range(1, ORDER - 1):
                keep(b, 2 * ORDER + jnp.where(a == 0, 0, ORDER - 2) + b - 1)

        for u in range(bands):
            rows = sublane_groups_swapped([sums[b][u] for b in range(ORDER)])
            for k in range(ORDER):
                o_ref[ORDER * u + k, pl.ds(first, ORDER), :] = rows[k]
        return carry

    lax.fori_loop(0, ORDER, op_rows, 0)


kept = [8 * a + b for a in range(8) for b in (0, 7)] + [8 * a + b for a in (0, 7) for b in range(1, 7)]


def element_stage(v3, received, ops, mass, helm, previous, chunk, tiles, modes, first):
    count = received.shape[2] // COLS
    aliased = previous is not None
    in_specs = [
        pl.BlockSpec((modes, NP, LANES), lambda t, f: (first + f, 0, chunk * tiles + t)),
        pl.BlockSpec((ORDER, modes, COLS), lambda t, f: (t, 0, f)),
        pl.BlockSpec((NP, NP, LANES), lambda t, f: (0, 0, chunk * tiles + t)),
        pl.BlockSpec((ORDER, ORDER, LANES), lambda t, f: (0, 0, chunk * tiles + t)),
        pl.BlockSpec((modes, LANES), lambda t, f: (0, 0)),
    ]
    args = [v3, received, ops, mass, helm]
    if aliased:
        in_specs.append(pl.BlockSpec(memory_space=pl.ANY))
        args.append(previous)
    values = jax.ShapeDtypeStruct((count * modes, tiles * PERIM * LANES), jnp.bfloat16)
    values_spec = pl.BlockSpec((modes, PERIM * LANES), lambda t, f: (f, t))
    return pl.pallas_call(
        functools.partial(element_kernel, modes, aliased),
        out_shape=(jax.ShapeDtypeStruct(v3.shape, jnp.float32), values, values),
        grid=(tiles, count),
        in_specs=in_specs,
        out_specs=(
            pl.BlockSpec((modes, NP, LANES), lambda t, f: (first + f, 0, chunk * tiles + t)),
            values_spec,
            values_spec,
        ),
        scratch_shapes=[pltpu.VMEM((NP, modes, LANES), jnp.float32)],
        input_output_aliases={5: 0} if aliased else {},
        compiler_params=pltpu.CompilerParams(vmem_limit_bytes=50 << 20),
        cost_estimate=pl.CostEstimate(
            flops=2 * count * tiles * modes * NP * NP * LANES, transcendentals=0,
            bytes_accessed=4 * 4 * count * tiles * modes * NP * LANES,
        ),
        name="element",
    )(*args)


def assemble_kernel(parts, block, *refs):
    ids_ref, o_ref = refs[2 * parts], refs[-1]
    rows, depth = o_ref.shape[0], refs[0].shape[1]
    wanted = lax.broadcasted_iota(jnp.int32, (WIDE, LANES), 1) + pl.program_id(0) * block
    total = jnp.zeros((2 * rows, block), jnp.float32)
    for start in range(0, depth, WIDE):
        ids = ids_ref[start : start + WIDE, :] - wanted
        hot = [jnp.where(ids == LANES * h, 1.0, 0.0).astype(jnp.bfloat16) for h in range(block // LANES)]
        values = jnp.concatenate([ref[:, start : start + WIDE] for ref in refs[: 2 * parts]], axis=0)
        total = total + dot(values, jnp.concatenate(hot, axis=1))
    total = total[:rows] + total[rows:]
    o_ref[...] = total if len(refs) == 2 * parts + 2 else refs[-2][...] + total


def assemble(values, ids, before, width, block=ASSEMBLED):
    highs, lows = zip(*values)
    rows, depth = sum(high.shape[0] for high in highs), highs[0].shape[1]
    in_specs = [pl.BlockSpec(memory_space=pltpu.VMEM)] * (2 * len(values) + 1)
    args = [*highs, *lows, ids]
    if before is not None:
        in_specs.append(pl.BlockSpec((rows, block), lambda n: (0, n)))
        args.append(before)
    return pl.pallas_call(
        functools.partial(assemble_kernel, len(values), block),
        out_shape=jax.ShapeDtypeStruct((rows, width), jnp.float32),
        grid=(width // block,),
        in_specs=in_specs,
        out_specs=pl.BlockSpec((rows, block), lambda n: (0, n)),
        compiler_params=pltpu.CompilerParams(vmem_limit_bytes=32 << 20),
        cost_estimate=pl.CostEstimate(
            flops=4 * rows * depth * width, transcendentals=0, bytes_accessed=4 * (2 * rows + LANES) * depth
        ),
        name="assemble",
    )(*args)


def split_blocks_kernel(b_ref, o_ref):
    for q in range(b_ref.shape[0]):
        for s in range(b_ref.shape[1]):
            rows = slice(s * LANES, (s + 1) * LANES)
            high, low = split(b_ref[q, s].T)
            o_ref[q, rows, :LANES] = high
            o_ref[q, rows, LANES:] = low


def split_blocks(blocks):
    count, slots, size, _ = blocks.shape
    pair = 2
    return pl.pallas_call(
        split_blocks_kernel,
        out_shape=jax.ShapeDtypeStruct((count, slots * size, 2 * size), jnp.bfloat16),
        grid=(count // pair,),
        in_specs=[pl.BlockSpec((pair, slots, size, size), lambda n: (n, 0, 0, 0))],
        out_specs=pl.BlockSpec((pair, slots * size, 2 * size), lambda n: (n, 0, 0)),
        compiler_params=pltpu.CompilerParams(vmem_limit_bytes=32 << 20),
        cost_estimate=pl.CostEstimate(
            flops=0, transcendentals=0, bytes_accessed=8 * count * slots * size * size
        ),
        name="split_blocks",
    )(blocks)


def coupling_kernel(cols_ref, at_ref, x_ref, w_ref, *refs):
    o_ref, both_ref = refs[-2:]
    step = pl.program_id(0)
    rows = x_ref.shape[0]
    group = w_ref.shape[0]
    slots = w_ref.shape[1] // LANES

    @pl.when(step == 0)
    def _():
        high, low = split(x_ref[...])
        both_ref[:rows] = high
        both_ref[rows:] = low

    for q in range(group):
        r = at_ref[step] * group + q
        picks = [pl.ds(pl.multiple_of(cols_ref[r, s] * LANES, LANES), LANES) for s in range(slots)]
        total = dot(jnp.concatenate([both_ref[:, at] for at in picks], axis=1), w_ref[q])
        total = total[:rows] + total[rows:]
        o_ref[:, q * LANES : (q + 1) * LANES] = total[:, :LANES] + total[:, LANES:]


def coupling(extended, local_cols, weights, order, group, previous):
    rows = extended.shape[0]
    count, depth, both = weights.shape
    in_specs = [
        pl.BlockSpec(extended.shape, lambda n, c, at: (0, 0)),
        pl.BlockSpec((group, depth, both), lambda n, c, at: (at[n], 0, 0)),
    ]
    args = [extended, weights]
    if previous is not None:
        in_specs.append(pl.BlockSpec(memory_space=pl.ANY))
        args.append(previous)
    return pl.pallas_call(
        coupling_kernel,
        out_shape=jax.ShapeDtypeStruct((rows, count * LANES), jnp.float32),
        grid_spec=pltpu.PrefetchScalarGridSpec(
            num_scalar_prefetch=2,
            grid=(len(order),),
            in_specs=in_specs,
            out_specs=pl.BlockSpec((rows, group * LANES), lambda n, c, at: (0, at[n])),
            scratch_shapes=[pltpu.VMEM((2 * rows, extended.shape[1]), jnp.bfloat16)],
        ),
        input_output_aliases={4: 0} if previous is not None else {},
        compiler_params=pltpu.CompilerParams(vmem_limit_bytes=32 << 20),
        cost_estimate=pl.CostEstimate(
            flops=4 * rows * depth * both * group * len(order), transcendentals=0,
            bytes_accessed=2 * depth * both * group * len(order),
        ),
        name="coupling",
    )(local_cols, jnp.asarray(order, jnp.int32), *args)


def swapped(value, earlier):
    if earlier:
        value, earlier[-1] = lax.optimization_barrier((value, earlier[-1]))
    return lax.all_to_all(value, "fourier", split_axis=0, concat_axis=0, tiled=True)


def per_device(velocity, metrics, lumped_mass, element_ops, boundary_map, block_cols, schur_blocks):
    modes, elems = velocity.shape[1], velocity.shape[3]
    groups = lax.axis_size("fourier")
    part = lax.axis_index("fourier")
    slab = lax.axis_index("mer")
    slabs = lax.axis_size("mer")
    block_rows, block_size = schur_blocks.shape[0], schur_blocks.shape[2]
    owned_count = block_rows * block_size
    tiles = groups // ORDER
    chunks = elems // (tiles * LANES)

    v3 = velocity.reshape(3 * modes, NP, elems)
    mass = lumped_mass.reshape(ORDER, ORDER, elems)
    wave = jnp.asarray(spectral_tables(K)[3], jnp.float32)
    local_wave = lax.dynamic_slice_in_dim(wave, part * modes, modes)
    helm = 1.0 + 4.0 * (local_wave / (K / 2)) ** 2
    helm = jnp.broadcast_to(helm[:, None], (modes, LANES))
    order = np.argsort(np.argsort(kept))
    ids = jnp.stack([boundary_map[:, n] for n in order], axis=1) - slab * owned_count
    ids = ids.reshape(chunks, tiles, LANES, PERIM).transpose(0, 1, 3, 2).reshape(chunks, -1)
    ids = jnp.broadcast_to(ids[:, :, None], ids.shape + (LANES,))
    width = -(-(owned_count + block_size) // ASSEMBLED) * ASSEMBLED

    me = jnp.reshape(part, (1,))
    arrived, source = [], v3
    for chunk in range(chunks):
        got = permuted(pack(source, me, chunk, tiles, modes, groups))
        if chunk + 1 < chunks:
            source, got[1] = lax.optimization_barrier((v3, got[1]))
        arrived.append(got)

    for now, later in zip(arrived, arrived[1:]):
        now[0], later[1] = lax.optimization_barrier((now[0], later[1]))

    projected, order = [], []
    for chunk in range(chunks):
        first = (chunk * tiles + part // ORDER) * LANES + (part % ORDER) * SUB
        local_metrics = lax.dynamic_slice_in_dim(metrics, first, SUB, 2).reshape(4 * ORDER, LANES)
        counts = (3,) if chunk + 1 < chunks else (2, 1)
        pieces = physics(arrived[chunk], me, part % ORDER, local_metrics, counts)
        projected.append([piece.reshape(groups, modes, piece.shape[1]) for piece in pieces])
        if chunk + 1 < chunks:
            both = (projected[chunk][0], arrived[chunk + 1])
            projected[chunk][0], arrived[chunk + 1] = lax.optimization_barrier(both)
        else:
            weights, projected[chunk] = lax.optimization_barrier((schur_blocks, projected[chunk]))
            early = (projected[chunk][0], split_blocks(weights))
            projected[chunk][0], weights = lax.optimization_barrier(early)
        order = [swapped(projected[chunk][0], order)]
        projected[chunk][0] = order[0]

    out, sums = None, None
    for chunk in range(chunks):
        values, first = [], 0
        if chunk + 1 == chunks:
            last = projected[chunk]
            if sums is not None:
                last[1], sums = lax.optimization_barrier((last[1], sums))
            last[1] = swapped(last[1], last[:1])
        for back in projected[chunk]:
            out, high, low = element_stage(
                v3, back, element_ops, mass, helm, out, chunk, tiles, modes, first
            )
            values.append((high, low))
            first += back.shape[2] // COLS
        sums = assemble(values, ids[chunk], sums, width)

    reach = HB * block_size
    up = [(i, i + 1) for i in range(slabs - 1)]
    down = [(i + 1, i) for i in range(slabs - 1)]
    from_below = lax.ppermute(sums[:, owned_count - reach : owned_count + block_size], "mer", up)
    from_above = lax.ppermute(sums[:, :reach], "mer", down)
    start = sums[:, :block_size] + from_below[:, reach:]
    after = from_above[:, :block_size] + sums[:, owned_count : owned_count + block_size]
    extended = jnp.concatenate(
        [from_below[:, :reach], start, sums[:, block_size:owned_count], after, from_above[:, block_size:]], axis=1
    )
    local_cols = block_cols - slab * block_rows
    inner = range(2 * HB, block_rows - HB)
    group = max(n for n in (4, 2) if len(inner) % n == 0 and inner.start % n == 0)
    inner = range(inner.start // group, inner.stop // group)
    outer = (*range(HB), block_rows // HB - 1)
    boundary_out = coupling(sums, local_cols, weights, inner, group, None)
    boundary_out = coupling(extended, local_cols + HB, weights, outer, HB, boundary_out)
    return (out.reshape(velocity.shape), boundary_out.reshape(3, modes, owned_count))


def solution(mesh):
    in_specs = (
        P(None, "fourier", None, "mer"),
        P(None, None, "mer"),
        P(None, "mer"),
        P(None, None, "mer"),
        P("mer", None),
        P("mer", None),
        P("mer", None, None, None),
    )
    out_specs = (P(None, "fourier", None, "mer"), P(None, "fourier", "mer"))
    return jax.shard_map(
        per_device, mesh=mesh, in_specs=in_specs, out_specs=out_specs, check_vma=False
    )
```

```python
import functools

import jax
import jax.numpy as jnp
import numpy as np
from jax import lax
from jax.experimental import pallas as pl
from jax.experimental.pallas import tpu as pltpu
from jax.sharding import PartitionSpec as P

K = 256
HB = 2
NP = 64
ORDER = 8
LANES = 128
SUB = LANES // ORDER
WIDE = 256
COLS = NP * SUB
PERIM = 28
VMEM_LIMIT = 61 << 20
ASSEMBLED = 1792


gauss_nodes = [
    -1.0,
    -0.8717401485096066,
    -0.5917001814331423,
    -0.2092992179024789,
    0.2092992179024789,
    0.5917001814331423,
    0.8717401485096066,
    1.0,
]
wave_scale = 1.0 / 32.0


def node_matrix():
    nodes = np.array(gauss_nodes)
    count = nodes.shape[0]
    barycentric = np.array(
        [1.0 / np.prod([nodes[i] - nodes[k] for k in range(count) if k != i]) for i in range(count)]
    )
    matrix = np.zeros((count, count))
    for i in range(count):
        for j in range(count):
            if i != j:
                matrix[i, j] = barycentric[j] / barycentric[i] / (nodes[i] - nodes[j])
        matrix[i, i] = -np.sum(matrix[i])
    return matrix


def spectral_tables(modes):
    planes = 3 * modes // 2
    index = np.arange(modes)
    wave = np.where(index == modes - 1, modes // 2, (index + 1) // 2)
    is_sine = (index % 2 == 0) & (index > 0) & (index < modes - 1)
    theta = 2.0 * np.pi * np.arange(planes) / planes
    angle = theta[:, None] * wave[None, :]
    basis = np.where(is_sine[None, :], np.sin(angle), np.cos(angle))
    deriv = wave_scale * wave[None, :] * np.where(is_sine[None, :], np.cos(angle), -np.sin(angle))
    weight = np.where(index == 0, 1.0, 2.0) / planes
    back = (basis * weight[None, :]).T
    return (basis, deriv, back, wave)


def halves(table):
    table = np.asarray(table, np.float32)
    high = table.astype(jnp.bfloat16)
    low = (table - high.astype(np.float32)).astype(jnp.bfloat16)
    return jnp.asarray(high), jnp.asarray(low)


def split(value):
    high = value.astype(jnp.bfloat16)
    low = (value - high.astype(jnp.float32)).astype(jnp.bfloat16)
    return high, low


def dot(left, right):
    return jnp.dot(left, right, preferred_element_type=jnp.float32)


def dot_nt(left, right):
    return lax.dot_general(left, right, (((1,), (1,)), ((), ())), preferred_element_type=jnp.float32)


def groups_picked(rows):
    lane = lax.broadcasted_iota(jnp.int32, rows[0].shape, 1)
    for step in (4, 2, 1):
        upper = (lane & (step * SUB)) != 0
        rows = [jnp.where(upper, rows[(i + step) % ORDER], rows[i]) for i in range(ORDER)]
    return [rows[-g % ORDER] for g in range(ORDER)]


def rolled(row, groups):
    shift = groups % ORDER * SUB
    return pltpu.roll(row, shift, 1) if shift else row


def sublane_groups_swapped(rows):
    rows = list(rows)
    line = lax.broadcasted_iota(jnp.int32, (ORDER, LANES), 0)
    for step in (4, 2, 1):
        lower = (line & step) == 0
        for i in range(ORDER):
            if i & step:
                continue
            top, bottom = rows[i], rows[i + step]
            rows[i] = jnp.where(lower, top, pltpu.roll(bottom, step, 0))
            rows[i + step] = jnp.where(lower, pltpu.roll(top, ORDER - step, 0), bottom)
    return rows


def partner_order(groups):
    return [0, 1] + sorted(range(2, groups), key=lambda s: (-bin(s >> 1).count("1"), s & 1, s))


def partners_swapped(rows, me):
    rows = list(rows)
    bit = 1
    while bit < len(rows):
        swap = (jnp.zeros(rows[0].shape, jnp.int32) + (me & bit)) != 0
        for i in range(len(rows)):
            if i & bit:
                continue
            top, bottom = rows[i], rows[i + bit]
            rows[i] = jnp.where(swap, bottom, top)
            rows[i + bit] = jnp.where(swap, top, bottom)
        bit *= 2
    return rows


def pack_kernel(modes, tiles, me_ref, v_ref, *o_refs):
    me = me_ref[0]
    for a in range(ORDER):
        pieces = []
        for t in range(tiles):
            lanes = slice(t * LANES, (t + 1) * LANES)
            bands = [
                sublane_groups_swapped([v_ref[u + k, a * ORDER : (a + 1) * ORDER, lanes] for k in range(ORDER)])
                for u in range(0, modes, ORDER)
            ]
            rows = [jnp.concatenate(band, axis=0) for band in zip(*bands)]
            pieces += groups_picked([rolled(row, b) for b, row in enumerate(rows)])
        pieces = partners_swapped(pieces, me)
        for o_ref, s in zip(o_refs, partner_order(len(o_refs))):
            o_ref[:, a * LANES : (a + 1) * LANES] = pieces[s]


def pack(v3, me, chunk, tiles, modes, groups):
    return pl.pallas_call(
        functools.partial(pack_kernel, modes, tiles),
        out_shape=[jax.ShapeDtypeStruct((modes, 3 * COLS), jnp.float32)] * groups,
        grid_spec=pltpu.PrefetchScalarGridSpec(
            num_scalar_prefetch=1,
            grid=(3,),
            in_specs=[pl.BlockSpec((modes, NP, tiles * LANES), lambda f, m: (f, 0, chunk))],
            out_specs=[pl.BlockSpec((modes, COLS), lambda f, m: (0, f))] * groups,
        ),
        compiler_params=pltpu.CompilerParams(vmem_limit_bytes=VMEM_LIMIT),
        cost_estimate=pl.CostEstimate(flops=0, transcendentals=0, bytes_accessed=8 * 3 * tiles * modes * NP * LANES),
        name="pack",
    )(me, v3)


def permuted(pieces):
    groups = len(pieces)
    return [
        lax.ppermute(piece, "fourier", [(i, i ^ s) for i in range(groups)]) if s else piece
        for s, piece in zip(partner_order(groups), pieces)
    ]


def physics_kernel(planes, even, odd, groups, counts, me_ref, fh_ref, fl_ref, wh_ref, wl_ref, bh_ref, bl_ref, m_ref,
                   *refs):
    pieces, outs = refs[:groups], refs[groups : groups + len(counts)]
    x_ref, y_ref, p_ref, z_ref, s_ref, ah_ref, al_ref, in_sem, out_sem = refs[groups + len(counts) :]
    modes = K // groups
    width = 3 * COLS

    arriving = []
    for n, partner in enumerate(partner_order(groups)):
        rows = pl.ds(pl.multiple_of((me_ref[0] ^ partner) * modes, modes), modes)
        arriving.append(pltpu.make_async_copy(pieces[n], x_ref.at[rows, :], in_sem.at[n]))
        arriving[n].start()
    for copy in arriving:
        copy.wait()

    def forward(tile, carry):
        cols = pl.ds(pl.multiple_of(tile * WIDE, WIDE), WIDE)
        xh, xl = split(x_ref[:, cols])
        fh = fh_ref[...]
        both = dot(fh, xh) + dot(fl_ref[...], xh) + dot(fh, xl)
        values = both[:planes]
        p_ref[:, cols] = values
        z_ref[:, cols] = both[planes:]
        ph, plo = split(values)
        wh = wh_ref[...]
        s_ref[:, cols] = dot(ph, wh) + dot(plo, wh) + dot(ph, wl_ref[...])
        return carry

    lax.fori_loop(0, width // WIDE, forward, 0)

    step = 16

    def products(tile, carry):
        rows = pl.ds(pl.multiple_of(tile * step, step), step)

        def piece(ref, f, a):
            start = f * COLS + a * LANES
            return ref[rows, start : start + LANES]

        speed_r, speed_s, speed_z = [], [], []
        for a in range(ORDER):
            p0, p1, p2 = (piece(p_ref, f, a) for f in range(3))
            m0, m1, m2, m3 = (m_ref[ORDER * q + a : ORDER * q + a + 1, :] for q in range(4))
            speed_r.append(p0 * m0 + p1 * m1)
            speed_s.append(p0 * m2 + p1 * m3)
            speed_z.append(p2)
        for f in range(3):
            values = [piece(p_ref, f, a) for a in range(ORDER)]
            total = [values[j] + values[7 - j] for j in range(4)]
            diff = [values[j] - values[7 - j] for j in range(4)]
            for i in range(4):
                e = even[i][0] * total[0]
                o = odd[i][0] * diff[0]
                for j in range(1, 4):
                    e = e + even[i][j] * total[j]
                    o = o + odd[i][j] * diff[j]
                for a, along in ((i, o + e), (7 - i, o - e)):
                    out = speed_r[a] * along + speed_s[a] * piece(s_ref, f, a) + speed_z[a] * piece(z_ref, f, a)
                    high, low = split(out)
                    start = f * COLS + a * LANES
                    ah_ref[rows, start : start + LANES] = high
                    al_ref[rows, start : start + LANES] = low
        return carry

    lax.fori_loop(0, planes // step, products, 0)

    def backward(tile, carry):
        cols = pl.ds(pl.multiple_of(tile * WIDE, WIDE), WIDE)
        ah = ah_ref[:, cols]
        bh = bh_ref[...]
        y_ref[:, cols] = dot(bh, ah) + dot(bl_ref[...], ah) + dot(bh, al_ref[:, cols])
        return carry

    start, leaving = 0, []
    for n, count in enumerate(counts):
        stop = start + count * COLS
        lax.fori_loop(start // WIDE, stop // WIDE, backward, 0)
        leaving.append(pltpu.make_async_copy(y_ref.at[:, start:stop], outs[n], out_sem.at[n]))
        leaving[-1].start()
        start = stop
    for copy in leaving:
        copy.wait()


def physics(received, me, turn, metrics, counts):
    groups = len(received)
    basis, deriv, back, _ = spectral_tables(K)
    planes = basis.shape[0]
    width = 3 * COLS
    fh, fl = halves(np.concatenate([basis, deriv], axis=0))
    bh, bl = halves(-back)
    matrix = node_matrix()
    metrics = jnp.roll(metrics, turn * SUB, 1)
    wh, wl = (jnp.roll(table, (turn, turn), (0, 1)) for table in halves(matrix.T))
    spread = [jnp.eye(n, dtype=jnp.bfloat16) for n in (WIDE // LANES, SUB)]
    wh, wl = (
        jnp.einsum("xy,bc,ef->xbeycf", spread[0], table, spread[1]).reshape(WIDE, WIDE) for table in (wh, wl)
    )
    flipped = matrix[:, ::-1]
    even = ((matrix + flipped) / 2)[:4, :4].astype(np.float32).tolist()
    odd = ((matrix - flipped) / 2)[:4, :4].astype(np.float32).tolist()
    return pl.pallas_call(
        functools.partial(physics_kernel, planes, even, odd, groups, counts),
        out_shape=[jax.ShapeDtypeStruct((K, count * COLS), jnp.float32) for count in counts],
        in_specs=[pl.BlockSpec(memory_space=pltpu.SMEM)]
        + [pl.BlockSpec(memory_space=pltpu.VMEM)] * 7
        + [pl.BlockSpec(memory_space=pl.ANY)] * groups,
        out_specs=[pl.BlockSpec(memory_space=pl.ANY)] * len(counts),
        scratch_shapes=[pltpu.VMEM((K, width), jnp.float32)] * 2
        + [pltpu.VMEM((planes, width), jnp.float32)] * 3
        + [pltpu.VMEM((planes, width), jnp.bfloat16)] * 2
        + [pltpu.SemaphoreType.DMA((groups,)), pltpu.SemaphoreType.DMA((len(counts),))],
        compiler_params=pltpu.CompilerParams(vmem_limit_bytes=VMEM_LIMIT),
        cost_estimate=pl.CostEstimate(
            flops=6 * planes * width * (3 * K + WIDE), transcendentals=0, bytes_accessed=8 * K * width
        ),
        name="physics",
    )(me, fh, fl, wh, wl, bh, bl, metrics, *received)


def element_kernel(modes, aliased, v_ref, r_ref, a_ref, mass_ref, helm_ref, *refs):
    o_ref, high_ref, low_ref, f_ref = refs[1:] if aliased else refs
    bands = modes // ORDER
    for a in range(ORDER):
        rows = groups_picked([r_ref[g, :, a * LANES : (a + 1) * LANES] for g in range(ORDER)])
        rows = [rolled(row, -b) for b, row in enumerate(rows)]
        for u in range(bands):
            own = sublane_groups_swapped([v_ref[ORDER * u + k, a * ORDER : (a + 1) * ORDER, :] for k in range(ORDER)])
            for b in range(ORDER):
                f_ref[ORDER * a + b, ORDER * u : ORDER * (u + 1), :] = own[b] + rows[b][ORDER * u : ORDER * (u + 1), :]

    def op_rows(a, carry):
        first = pl.multiple_of(a * ORDER, ORDER)
        sums = []
        for b in range(ORDER):
            weight = helm_ref[...] * mass_ref[a, b : b + 1, :]
            own = f_ref[first + b]
            sums.append([(weight * own)[ORDER * u : ORDER * (u + 1), :] for u in range(bands)])
        for j in range(NP):
            value = f_ref[j]
            for b in range(ORDER):
                weight = a_ref[first + b, j : j + 1, :]
                for u in range(bands):
                    sums[b][u] = sums[b][u] + weight * value[ORDER * u : ORDER * (u + 1), :]

        def keep(b, slot):
            at = pl.ds(pl.multiple_of(slot * LANES, LANES), LANES)
            high, low = split(jnp.concatenate(sums[b], axis=0))
            high_ref[:, at] = high
            low_ref[:, at] = low

        keep(0, 2 * a)
        keep(ORDER - 1, 2 * a + 1)

        @pl.when((a == 0) | (a == ORDER - 1))
        def _():
            for b in range(1, ORDER - 1):
                keep(b, 2 * ORDER + jnp.where(a == 0, 0, ORDER - 2) + b - 1)

        for u in range(bands):
            rows = sublane_groups_swapped([sums[b][u] for b in range(ORDER)])
            for k in range(ORDER):
                o_ref[ORDER * u + k, pl.ds(first, ORDER), :] = rows[k]
        return carry

    lax.fori_loop(0, ORDER, op_rows, 0)


kept = [8 * a + b for a in range(8) for b in (0, 7)] + [8 * a + b for a in (0, 7) for b in range(1, 7)]


def element_stage(v3, received, ops, mass, helm, previous, chunk, tiles, modes, first):
    count = received.shape[2] // COLS
    aliased = previous is not None
    in_specs = [
        pl.BlockSpec((modes, NP, LANES), lambda t, f: (first + f, 0, chunk * tiles + t)),
        pl.BlockSpec((ORDER, modes, COLS), lambda t, f: (t, 0, f)),
        pl.BlockSpec((NP, NP, LANES), lambda t, f: (0, 0, chunk * tiles + t)),
        pl.BlockSpec((ORDER, ORDER, LANES), lambda t, f: (0, 0, chunk * tiles + t)),
        pl.BlockSpec((modes, LANES), lambda t, f: (0, 0)),
    ]
    args = [v3, received, ops, mass, helm]
    if aliased:
        in_specs.append(pl.BlockSpec(memory_space=pl.ANY))
        args.append(previous)
    values = jax.ShapeDtypeStruct((count * modes, tiles * PERIM * LANES), jnp.bfloat16)
    values_spec = pl.BlockSpec((modes, PERIM * LANES), lambda t, f: (f, t))
    return pl.pallas_call(
        functools.partial(element_kernel, modes, aliased),
        out_shape=(jax.ShapeDtypeStruct(v3.shape, jnp.float32), values, values),
        grid=(tiles, count),
        in_specs=in_specs,
        out_specs=(
            pl.BlockSpec((modes, NP, LANES), lambda t, f: (first + f, 0, chunk * tiles + t)),
            values_spec,
            values_spec,
        ),
        scratch_shapes=[pltpu.VMEM((NP, modes, LANES), jnp.float32)],
        input_output_aliases={5: 0} if aliased else {},
        compiler_params=pltpu.CompilerParams(vmem_limit_bytes=50 << 20),
        cost_estimate=pl.CostEstimate(
            flops=2 * count * tiles * modes * NP * NP * LANES, transcendentals=0,
            bytes_accessed=4 * 4 * count * tiles * modes * NP * LANES,
        ),
        name="element",
    )(*args)


def assemble_kernel(parts, block, *refs):
    ids_ref, o_ref = refs[2 * parts], refs[-1]
    rows, depth = o_ref.shape[0], refs[0].shape[1]
    wanted = lax.broadcasted_iota(jnp.int32, (WIDE, LANES), 1) + pl.program_id(0) * block
    total = jnp.zeros((2 * rows, block), jnp.float32)
    for start in range(0, depth, WIDE):
        ids = ids_ref[start : start + WIDE, :] - wanted
        hot = [jnp.where(ids == LANES * h, 1.0, 0.0).astype(jnp.bfloat16) for h in range(block // LANES)]
        values = jnp.concatenate([ref[:, start : start + WIDE] for ref in refs[: 2 * parts]], axis=0)
        total = total + dot(values, jnp.concatenate(hot, axis=1))
    total = total[:rows] + total[rows:]
    o_ref[...] = total if len(refs) == 2 * parts + 2 else refs[-2][...] + total


def assemble(values, ids, before, width, block=ASSEMBLED):
    highs, lows = zip(*values)
    rows, depth = sum(high.shape[0] for high in highs), highs[0].shape[1]
    in_specs = [pl.BlockSpec(memory_space=pltpu.VMEM)] * (2 * len(values) + 1)
    args = [*highs, *lows, ids]
    if before is not None:
        in_specs.append(pl.BlockSpec((rows, block), lambda n: (0, n)))
        args.append(before)
    return pl.pallas_call(
        functools.partial(assemble_kernel, len(values), block),
        out_shape=jax.ShapeDtypeStruct((rows, width), jnp.float32),
        grid=(width // block,),
        in_specs=in_specs,
        out_specs=pl.BlockSpec((rows, block), lambda n: (0, n)),
        compiler_params=pltpu.CompilerParams(vmem_limit_bytes=32 << 20),
        cost_estimate=pl.CostEstimate(
            flops=4 * rows * depth * width, transcendentals=0, bytes_accessed=4 * (2 * rows + LANES) * depth
        ),
        name="assemble",
    )(*args)


def split_blocks_kernel(b_ref, o_ref):
    for q in range(b_ref.shape[0]):
        for s in range(b_ref.shape[1]):
            rows = slice(s * LANES, (s + 1) * LANES)
            high, low = split(b_ref[q, s].T)
            o_ref[q, rows, :LANES] = high
            o_ref[q, rows, LANES:] = low


def split_blocks(blocks):
    count, slots, size, _ = blocks.shape
    pair = 2
    return pl.pallas_call(
        split_blocks_kernel,
        out_shape=jax.ShapeDtypeStruct((count, slots * size, 2 * size), jnp.bfloat16),
        grid=(count // pair,),
        in_specs=[pl.BlockSpec((pair, slots, size, size), lambda n: (n, 0, 0, 0))],
        out_specs=pl.BlockSpec((pair, slots * size, 2 * size), lambda n: (n, 0, 0)),
        compiler_params=pltpu.CompilerParams(vmem_limit_bytes=32 << 20),
        cost_estimate=pl.CostEstimate(
            flops=0, transcendentals=0, bytes_accessed=8 * count * slots * size * size
        ),
        name="split_blocks",
    )(blocks)


def coupling_kernel(cols_ref, at_ref, x_ref, w_ref, *refs):
    o_ref, both_ref = refs[-2:]
    step = pl.program_id(0)
    rows = x_ref.shape[0]
    group = w_ref.shape[0]
    slots = w_ref.shape[1] // LANES

    @pl.when(step == 0)
    def _():
        high, low = split(x_ref[...])
        both_ref[:rows] = high
        both_ref[rows:] = low

    for q in range(group):
        r = at_ref[step] * group + q
        picks = [pl.ds(pl.multiple_of(cols_ref[r, s] * LANES, LANES), LANES) for s in range(slots)]
        total = dot(jnp.concatenate([both_ref[:, at] for at in picks], axis=1), w_ref[q])
        total = total[:rows] + total[rows:]
        o_ref[:, q * LANES : (q + 1) * LANES] = total[:, :LANES] + total[:, LANES:]


def coupling(extended, local_cols, weights, order, group, previous):
    rows = extended.shape[0]
    count, depth, both = weights.shape
    in_specs = [
        pl.BlockSpec(extended.shape, lambda n, c, at: (0, 0)),
        pl.BlockSpec((group, depth, both), lambda n, c, at: (at[n], 0, 0)),
    ]
    args = [extended, weights]
    if previous is not None:
        in_specs.append(pl.BlockSpec(memory_space=pl.ANY))
        args.append(previous)
    return pl.pallas_call(
        coupling_kernel,
        out_shape=jax.ShapeDtypeStruct((rows, count * LANES), jnp.float32),
        grid_spec=pltpu.PrefetchScalarGridSpec(
            num_scalar_prefetch=2,
            grid=(len(order),),
            in_specs=in_specs,
            out_specs=pl.BlockSpec((rows, group * LANES), lambda n, c, at: (0, at[n])),
            scratch_shapes=[pltpu.VMEM((2 * rows, extended.shape[1]), jnp.bfloat16)],
        ),
        input_output_aliases={4: 0} if previous is not None else {},
        compiler_params=pltpu.CompilerParams(vmem_limit_bytes=32 << 20),
        cost_estimate=pl.CostEstimate(
            flops=4 * rows * depth * both * group * len(order), transcendentals=0,
            bytes_accessed=2 * depth * both * group * len(order),
        ),
        name="coupling",
    )(local_cols, jnp.asarray(order, jnp.int32), *args)


def swapped(value, earlier):
    if earlier:
        value, earlier[-1] = lax.optimization_barrier((value, earlier[-1]))
    return lax.all_to_all(value, "fourier", split_axis=0, concat_axis=0, tiled=True)


def per_device(velocity, metrics, lumped_mass, element_ops, boundary_map, block_cols, schur_blocks):
    modes, elems = velocity.shape[1], velocity.shape[3]
    groups = lax.axis_size("fourier")
    part = lax.axis_index("fourier")
    slab = lax.axis_index("mer")
    slabs = lax.axis_size("mer")
    block_rows, block_size = schur_blocks.shape[0], schur_blocks.shape[2]
    owned_count = block_rows * block_size
    tiles = groups // ORDER
    chunks = elems // (tiles * LANES)

    v3 = velocity.reshape(3 * modes, NP, elems)
    mass = lumped_mass.reshape(ORDER, ORDER, elems)
    wave = jnp.asarray(spectral_tables(K)[3], jnp.float32)
    local_wave = lax.dynamic_slice_in_dim(wave, part * modes, modes)
    helm = 1.0 + 4.0 * (local_wave / (K / 2)) ** 2
    helm = jnp.broadcast_to(helm[:, None], (modes, LANES))
    order = np.argsort(np.argsort(kept))
    ids = jnp.stack([boundary_map[:, n] for n in order], axis=1) - slab * owned_count
    ids = ids.reshape(chunks, tiles, LANES, PERIM).transpose(0, 1, 3, 2).reshape(chunks, -1)
    ids = jnp.broadcast_to(ids[:, :, None], ids.shape + (LANES,))
    width = -(-(owned_count + block_size) // ASSEMBLED) * ASSEMBLED

    me = jnp.reshape(part, (1,))
    arrived, source = [], v3
    for chunk in range(chunks):
        got = permuted(pack(source, me, chunk, tiles, modes, groups))
        if chunk + 1 < chunks:
            source, got[1] = lax.optimization_barrier((v3, got[1]))
        arrived.append(got)

    for now, later in zip(arrived, arrived[1:]):
        now[0], later[1] = lax.optimization_barrier((now[0], later[1]))

    projected, order = [], []
    for chunk in range(chunks):
        first = (chunk * tiles + part // ORDER) * LANES + (part % ORDER) * SUB
        local_metrics = lax.dynamic_slice_in_dim(metrics, first, SUB, 2).reshape(4 * ORDER, LANES)
        counts = (3,) if chunk + 1 < chunks else (2, 1)
        pieces = physics(arrived[chunk], me, part % ORDER, local_metrics, counts)
        projected.append([piece.reshape(groups, modes, piece.shape[1]) for piece in pieces])
        if chunk + 1 < chunks:
            both = (projected[chunk][0], arrived[chunk + 1])
            projected[chunk][0], arrived[chunk + 1] = lax.optimization_barrier(both)
        else:
            weights, projected[chunk] = lax.optimization_barrier((schur_blocks, projected[chunk]))
            early = (projected[chunk][0], split_blocks(weights))
            projected[chunk][0], weights = lax.optimization_barrier(early)
        order = [swapped(projected[chunk][0], order)]
        projected[chunk][0] = order[0]

    out, sums = None, None
    for chunk in range(chunks):
        values, first = [], 0
        if chunk + 1 == chunks:
            last = projected[chunk]
            if sums is not None:
                last[1], sums = lax.optimization_barrier((last[1], sums))
            last[1] = swapped(last[1], last[:1])
        for back in projected[chunk]:
            out, high, low = element_stage(
                v3, back, element_ops, mass, helm, out, chunk, tiles, modes, first
            )
            values.append((high, low))
            first += back.shape[2] // COLS
        sums = assemble(values, ids[chunk], sums, width)

    reach = HB * block_size
    up = [(i, i + 1) for i in range(slabs - 1)]
    down = [(i + 1, i) for i in range(slabs - 1)]
    from_below = lax.ppermute(sums[:, owned_count - reach : owned_count + block_size], "mer", up)
    from_above = lax.ppermute(sums[:, :reach], "mer", down)
    start = sums[:, :block_size] + from_below[:, reach:]
    after = from_above[:, :block_size] + sums[:, owned_count : owned_count + block_size]
    extended = jnp.concatenate(
        [from_below[:, :reach], start, sums[:, block_size:owned_count], after, from_above[:, block_size:]], axis=1
    )
    local_cols = block_cols - slab * block_rows
    inner = range(2 * HB, block_rows - HB)
    group = max(n for n in (4, 2) if len(inner) % n == 0 and inner.start % n == 0)
    inner = range(inner.start // group, inner.stop // group)
    outer = (*range(HB), block_rows // HB - 1)
    boundary_out = coupling(sums, local_cols, weights, inner, group, None)
    boundary_out = coupling(extended, local_cols + HB, weights, outer, HB, boundary_out)
    return (out.reshape(velocity.shape), boundary_out.reshape(3, modes, owned_count))


def solution(mesh):
    in_specs = (
        P(None, "fourier", None, "mer"),
        P(None, None, "mer"),
        P(None, "mer"),
        P(None, None, "mer"),
        P("mer", None),
        P("mer", None),
        P("mer", None, None, None),
    )
    out_specs = (P(None, "fourier", None, "mer"), P(None, "fourier", "mer"))
    return jax.shard_map(
        per_device, mesh=mesh, in_specs=in_specs, out_specs=out_specs, check_vma=False
    )
```
